32 devices in a mesh: geo: 8 (over z, y), rep: 4 (over x, core).
Axes of the slice: x: 2, y: 2, z: 4, core: 2. Of those that a mesh axis runs over, the one named last changes fastest.
Arguments:
- base: float32 [65536], P(('geo', 'rep')), may hold values from 0.5 to 2
- job_res: int32 [65536], P(('geo', 'rep')), may hold values from 0 to 255
- job_slot: int32 [65536], P(('geo', 'rep')), may hold values from 0 to 255
- job_cell: int32 [65536], P(('geo', 'rep')), may hold values from 0 to 29
- needed: int32 [8, 8, 1], P('geo'), may hold values from 0 to 7
- lam_res: float32 [30, 2048], P(None, 'geo'), may hold values from -2 to 2
- lam_work: float32 [30, 2048], P(None, 'geo'), may hold values from -2 to 2
- target_res: float32 [30, 2048], P(None, 'geo'), may hold values from 0.3 to 3
- target_work: float32 [30, 2048], P(None, 'geo'), may hold values from 0.3 to 3
Outputs:
- step_res: float32 [30, 2048], P(None, 'geo')
- step_work: float32 [30, 2048], P(None, 'geo')
- resid_res: float32 [30, 2048], P(None, 'geo')
- resid_work: float32 [30, 2048], P(None, 'geo')
The draws below stay inside these ranges and needn't reach their ends.
Inputs may be any that keep to these rules, and one draw needn't show every extreme that they name: needed[g, p, k] is a block of owner p's tracts; block b covers that owner's local tracts b * 32 to b * 32 + 31.
All inputs are finite; a program needn't handle non-finite values.
Results may differ from the reference program's by a relative error of at most 0.0003.
Values sent between devices are 32-bit elements; how exact they have to be, the bound alone decides.
No kernel may reach another device: no remote copies, remote signals or barrier semaphores. Data moves between devices by JAX's collectives and lax.ppermute only.
A program may use at most 64 MiB of HBM per device.

```python
import math
import jax
import jax.numpy as jnp

CELLS = 30
BLK = 32
CAP = 1
ITERS = 3
TR_DEV = 256
JOB_DEV = 2048
BLOCKS = 8
TRACTS = 2048
SLOTS = 256
JOBS = 65536
N_GEO = 8
N_REP = 4


def set_ends(result, key, least, high):
    spot = [jax.random.randint(jax.random.fold_in(key, axis), (), 0, length) for axis, length in enumerate(result.shape)]
    longest = result.shape.index(max(result.shape))
    beside = spot[:longest] + [(spot[longest] + 1) % result.shape[longest]] + spot[longest + 1:]
    return result.at[tuple(spot)].set(least).at[tuple(beside)].set(high)


def block_scale(key, shape, pieces, low, top_value):
    def one(position, blocks):
        heights = jax.random.uniform(jax.random.fold_in(jax.random.fold_in(key, 6), position), (blocks,), jnp.float32, low / len(pieces), top_value / len(pieces))
        return jnp.repeat(jnp.exp(heights), shape[position] // blocks).reshape((-1,) + (1,) * (len(shape) - position - 1))

    level = one(*pieces[0])
    for cut in pieces[1:]:
        level = level * one(*cut)
    return level


def normal_values(key, extent, width, most, cuts=(), kind=jnp.bfloat16):
    drawn = width * jax.random.normal(key, extent, jnp.float32)
    if cuts:
        drawn = drawn * block_scale(key, extent, cuts, -0.22, 0.18)
    return jnp.clip(drawn, -most, most).astype(kind)


def setup_inputs(seed: int = 0) -> dict:
    streams_of = jax.random.split(jax.random.key(seed), 10)
    return {
        "base": jnp.clip(jnp.exp(math.log(2.0) - 1.3862944 * jax.random.uniform(streams_of[0], (JOBS,), jnp.float32) ** block_scale(streams_of[0], (JOBS,), ((0, 32),), -0.2, 0.2)), 0.5, 2.0),
        "job_res": set_ends(jax.random.randint(streams_of[1], (JOBS,), 0, TR_DEV), jax.random.fold_in(streams_of[1], 1), 0, TR_DEV - 1).astype(jnp.int32),
        "job_slot": set_ends(jax.random.randint(streams_of[2], (JOBS,), 0, SLOTS), jax.random.fold_in(streams_of[2], 1), 0, SLOTS - 1).astype(jnp.int32),
        "job_cell": set_ends(jax.random.randint(streams_of[3], (JOBS,), 0, CELLS), jax.random.fold_in(streams_of[3], 1), 0, CELLS - 1).astype(jnp.int32),
        "needed": set_ends(jax.random.randint(streams_of[4], (N_GEO, N_GEO, CAP), 0, BLOCKS), jax.random.fold_in(streams_of[4], 1), 0, BLOCKS - 1).astype(jnp.int32),
        "lam_res": normal_values(streams_of[5], (CELLS, TRACTS), 0.3, 2.0, ((1, 8),), jnp.float32),
        "lam_work": normal_values(streams_of[6], (CELLS, TRACTS), 0.3, 2.0, ((1, 8),), jnp.float32),
        "target_res": jnp.clip(jnp.exp(math.log(3.0) - 2.3025851 * jax.random.uniform(streams_of[7], (CELLS, TRACTS), jnp.float32) ** block_scale(streams_of[7], (CELLS, TRACTS), ((1, 8),), -0.2, 0.2)), 0.3, 3.0),
        "target_work": jnp.clip(jnp.exp(math.log(3.0) - 2.3025851 * jax.random.uniform(streams_of[8], (CELLS, TRACTS), jnp.float32) ** block_scale(streams_of[8], (CELLS, TRACTS), ((1, 8),), -0.2, 0.2)), 0.3, 3.0),
    }


RIDGE = 0.5


def reference(base, job_res, job_slot, job_cell, needed, lam_res, lam_work, target_res, target_work):
    tracts = lam_res.shape[1]
    group = (jnp.arange(JOBS, dtype=jnp.int32) // (JOB_DEV * N_REP)).astype(jnp.int32)
    owner = (job_slot // (CAP * BLK)).astype(jnp.int32)
    within = ((job_slot // BLK) % CAP).astype(jnp.int32)
    block = needed[group, owner, within].astype(jnp.int32)
    res_tract = group * TR_DEV + job_res
    work_tract = owner * TR_DEV + block * BLK + job_slot % BLK
    res_index = (job_cell * tracts + res_tract).astype(jnp.int32)
    work_index = (job_cell * tracts + work_tract).astype(jnp.int32)
    weight = base * jnp.exp(lam_res.reshape(-1)[res_index] + lam_work.reshape(-1)[work_index])

    def totals(values):
        res_part = jax.ops.segment_sum(values, res_index, num_segments=CELLS * tracts).reshape(CELLS, tracts)
        work_part = jax.ops.segment_sum(values, work_index, num_segments=CELLS * tracts).reshape(CELLS, tracts)
        return res_part, work_part

    def inner(a_res, a_work, b_res, b_work):
        return jnp.sum(a_res * b_res) + jnp.sum(a_work * b_work)

    total_res, total_work = totals(weight)
    resid_res = -(total_res - target_res)
    resid_work = -(total_work - target_work)
    step_res = jnp.zeros_like(resid_res)
    step_work = jnp.zeros_like(resid_work)
    dir_res, dir_work = resid_res, resid_work
    norm_now = inner(resid_res, resid_work, resid_res, resid_work)
    for turn in range(ITERS):
        along = dir_res.reshape(-1)[res_index] + dir_work.reshape(-1)[work_index]
        image_res, image_work = totals(weight * along)
        image_res = image_res + RIDGE * dir_res
        image_work = image_work + RIDGE * dir_work
        alpha = norm_now / inner(dir_res, dir_work, image_res, image_work)
        step_res = step_res + alpha * dir_res
        step_work = step_work + alpha * dir_work
        resid_res = resid_res - alpha * image_res
        resid_work = resid_work - alpha * image_work
        norm_next = inner(resid_res, resid_work, resid_res, resid_work)
        dir_res = resid_res + (norm_next / norm_now) * dir_res
        dir_work = resid_work + (norm_next / norm_now) * dir_work
        norm_now = norm_next
    return (step_res, step_work, resid_res, resid_work)
```

```python
import functools

import jax
import jax.numpy as jnp
from jax import lax
from jax.experimental import pallas as pl
from jax.experimental.pallas import tpu as pltpu
from jax.sharding import PartitionSpec as P

BLK = 32
ITERS = 3
RIDGE = 0.5
LANES = 128
TABLE_BYTES = 8 << 20
ALL = ("geo", "rep")

F32 = jnp.float32
BF16 = jnp.bfloat16


def start_plan(base, job_res, job_slot, job_cell, needed, lam_res, lam_work, target_res, target_work):
    cells, tracts_dev = lam_res.shape
    blocks_dev = tracts_dev // BLK
    requests = lax.all_to_all(needed[0], "geo", split_axis=0, concat_axis=0, tiled=True)
    sources, listed = requests.shape
    onehot = (
        requests[:, :, None] == jnp.arange(blocks_dev, dtype=jnp.int32)[None, None, :]
    ).astype(jnp.float32)
    slot_shape = (sources, listed, cells, BLK)
    slot_count = sources * listed * cells * BLK
    res_index = job_cell * tracts_dev + job_res
    work_index = (job_slot // BLK * cells + job_cell) * BLK + job_slot % BLK

    def serve(table):
        blocks = table.reshape(cells, blocks_dev, BLK).transpose(1, 0, 2)
        return jnp.take(blocks, requests, axis=0)

    def pick(fetched):
        return fetched.reshape(-1)[work_index]

    def fold(arrived):
        return jnp.einsum("skb,skcx->cbx", onehot, arrived, precision=lax.Precision.HIGHEST)

    def totals(values):
        res_part = jax.ops.segment_sum(values, res_index, num_segments=cells * tracts_dev).reshape(
            cells, tracts_dev
        )
        work_part = jax.ops.segment_sum(values, work_index, num_segments=slot_count).reshape(
            slot_shape
        )
        arrived = lax.all_to_all(work_part, "geo", split_axis=0, concat_axis=0, tiled=True)
        folded = fold(arrived)
        return lax.psum((res_part, folded.reshape(cells, tracts_dev)), "rep")

    def inner(a_res, a_work, b_res, b_work):
        return lax.psum(jnp.sum(a_res * b_res) + jnp.sum(a_work * b_work), "geo")

    fetched_lam = lax.all_to_all(serve(lam_work), "geo", split_axis=0, concat_axis=0, tiled=True)
    weight = base * jnp.exp(lam_res.reshape(-1)[res_index] + pick(fetched_lam))
    total_res, total_work = totals(weight)
    resid_res = -(total_res - target_res)
    resid_work = -(total_work - target_work)
    norm = inner(resid_res, resid_work, resid_res, resid_work)
    zeros = jnp.zeros_like(resid_res)

    def turn(_, state):
        step_res, step_work, resid_res, resid_work, dir_res, dir_work, norm_now = state
        dir_piece = lax.all_to_all(serve(dir_work), "geo", split_axis=0, concat_axis=0, tiled=True)
        along = dir_res.reshape(-1)[res_index] + pick(dir_piece)
        image_res, image_work = totals(weight * along)
        image_res = image_res + RIDGE * dir_res
        image_work = image_work + RIDGE * dir_work
        alpha = norm_now / inner(dir_res, dir_work, image_res, image_work)
        step_res = step_res + alpha * dir_res
        step_work = step_work + alpha * dir_work
        resid_res = resid_res - alpha * image_res
        resid_work = resid_work - alpha * image_work
        norm_next = inner(resid_res, resid_work, resid_res, resid_work)
        dir_res = resid_res + norm_next / norm_now * dir_res
        dir_work = resid_work + norm_next / norm_now * dir_work
        return step_res, step_work, resid_res, resid_work, dir_res, dir_work, norm_next

    state = (zeros, zeros, resid_res, resid_work, resid_res, resid_work, norm)
    return lax.fori_loop(0, ITERS, turn, state)[:4]


def split2(x):
    high = x.astype(BF16)
    low = (x - high.astype(F32)).astype(BF16)
    return high, low


def split3(x):
    high = x.astype(BF16)
    rest = x - high.astype(F32)
    mid = rest.astype(BF16)
    low = (rest - mid.astype(F32)).astype(BF16)
    return high, mid, low


def dot_nt(a, b):
    return lax.dot_general(a, b, (((1,), (1,)), ((), ())), preferred_element_type=F32)


def dot_nn(a, b):
    return jnp.dot(a, b, preferred_element_type=F32)


def pack_kernel(dims, needed_ref, base_ref, res_ref, slot_ref, cell_ref, a_ref, b_ref, c_ref, d_ref, out_ref):
    devices, rows, cap, listed, cells = dims["devices"], dims["rows"], dims["cap"], dims["listed"], dims["cells"]
    tracts = a_ref.shape[1]
    jobs = cell_ref.shape[1]
    chunk = 256
    cell = cell_ref[...]
    member = lax.broadcasted_iota(jnp.int32, (devices, jobs), 0) == cell
    member_b = member.astype(F32).astype(BF16)
    before = lax.broadcasted_iota(jnp.int32, (chunk, chunk), 0) < lax.broadcasted_iota(jnp.int32, (chunk, chunk), 1)
    before = before.astype(F32).astype(BF16)
    ranks = []
    count = jnp.zeros((devices, 1), F32)
    for at in range(0, jobs, chunk):
        part = member_b[:, at : at + chunk]
        seen = dot_nn(part, before) + count
        own = member[:, at : at + chunk]
        ranks.append(jnp.sum(jnp.where(own, seen, 0.0), axis=0, keepdims=True))
        count = count + jnp.sum(own.astype(F32), axis=1, keepdims=True)
    rank = jnp.concatenate(ranks, axis=1).astype(jnp.int32)
    largest = jnp.max(count, axis=0, keepdims=True)
    chosen = lax.broadcasted_iota(jnp.int32, (cap, jobs), 0) == rank
    high, low = split2(base_ref[...])
    values = (res_ref[...].astype(F32), slot_ref[...].astype(F32), high.astype(F32), low.astype(F32))
    sent = [dot_nt(member_b, jnp.where(chosen, value, 0.0).astype(BF16)) for value in values]
    sent = (sent[0], sent[1], sent[2] + sent[3])

    def put(row, value):
        out_ref[pl.ds(row, devices, stride=rows), :] = value

    row = 0
    for value in sent:
        for at in range(0, cap, LANES):
            put(row, value[:, at : at + LANES])
            row += 1
    owner = lax.broadcasted_iota(jnp.int32, (devices, listed * BLK), 1) // BLK
    wanted = jnp.zeros((devices, listed * BLK), F32)
    for p in range(listed):
        wanted = jnp.where(owner == p, needed_ref[p].astype(F32), wanted)
    for at in range(0, listed * BLK, LANES):
        put(row, wanted[:, at : at + LANES])
        row += 1
    put(row, jnp.broadcast_to(largest, (devices, LANES)))
    row += 1
    rep = lax.axis_index("rep")
    mine = a_ref[...]
    for k, ref in enumerate((b_ref, c_ref, d_ref)):
        mine = jnp.where(rep == k + 1, ref[...], mine)
    mine = jnp.concatenate([mine, jnp.zeros((devices - cells, tracts), F32)], axis=0)
    for at in range(0, tracts, LANES):
        put(row, mine[:, at : at + LANES])
        row += 1


def swap_blocks(x):
    side, width = x.shape
    shift = (
        lax.broadcasted_iota(jnp.int32, (side, width), 0)
        - lax.broadcasted_iota(jnp.int32, (side, width), 1) // BLK
        + side
    ) % side
    out = x
    for d in range(1, side):
        moved = pltpu.roll(pltpu.roll(x, width - BLK * d, 1), d, 0)
        out = jnp.where(shift == d, moved, out)
    return out


def total(x):
    return jnp.sum(jnp.sum(x, axis=0, keepdims=True), axis=1, keepdims=True)


def cell_kernel(dims, in_ref, out_ref, flag_ref, hi_ref, lo_ref):
    devices, rows, cap, groups, reps, tracts, slots, sent_rows = (
        dims[k] for k in ("devices", "rows", "cap", "groups", "reps", "tracts", "slots", "sent_rows")
    )
    per = cap // LANES

    def row_of(row, device):
        return in_ref[pl.ds(device * rows + row, 1), :]

    def group_rows(row, rep):
        return in_ref[pl.ds(rep * rows + row, groups, stride=rows * reps), :]

    def wide(row, rep, width):
        return jnp.concatenate([group_rows(row + k, rep) for k in range(width // LANES)], axis=1)

    at_res, at_slot, at_base, at_need = 0, per, 2 * per, 3 * per
    at_most = at_need + slots // LANES
    at_own = at_most + 1

    tract = lax.broadcasted_iota(jnp.int32, (tracts, LANES), 0).astype(F32)
    place = lax.broadcasted_iota(jnp.int32, (slots, LANES), 0).astype(F32)
    for g in range(groups):
        highs, lows, picks = [], [], []
        for r in range(reps):
            for k in range(per):
                device = g * reps + r
                high, low = split2(row_of(at_base + k, device))
                at_tract = tract == row_of(at_res + k, device)
                highs.append(jnp.where(at_tract, high.astype(F32), 0.0).astype(BF16))
                lows.append(jnp.where(at_tract, low.astype(F32), 0.0).astype(BF16))
                picks.append((place == row_of(at_slot + k, device)).astype(F32).astype(BF16))
        picked = jnp.concatenate(picks, axis=1)
        table = dot_nt(jnp.concatenate(highs, axis=1), picked) + dot_nt(jnp.concatenate(lows, axis=1), picked)
        high, low = split2(table)
        hi_ref[g] = high
        lo_ref[g] = low

    need = wide(at_need, 0, slots)
    lam_res = wide(at_own, 0, tracts)
    lam_work = swap_blocks(wide(at_own, 1, tracts))
    target_res = wide(at_own, 2, tracts)
    target_work = swap_blocks(wide(at_own, 3, tracts))

    block_row = lax.broadcasted_iota(jnp.int32, (groups, slots), 0).astype(F32)

    def fetch(v):
        out = jnp.zeros((groups, slots), F32)
        for b in range(groups):
            out = jnp.where(need == float(b), v[b : b + 1, :], out)
        return out

    def fold(u):
        out = jnp.zeros((groups, slots), F32)
        for g in range(groups):
            out = out + jnp.where(need[g : g + 1, :] == block_row, u[g : g + 1, :], 0.0)
        return out

    rise_res = jnp.exp(lam_res)
    rise_work = jnp.exp(fetch(lam_work))
    group_row = lax.broadcasted_iota(jnp.int32, (3 * groups, tracts), 0) % groups

    def spread(x):
        return jnp.concatenate([piece.astype(F32) for piece in split3(x)], axis=0)

    def across(u_res, u_list):
        left = spread(rise_work * u_list)
        right = spread(rise_res * u_res)
        to_res = jnp.zeros((3 * groups, tracts), F32)
        to_list = jnp.zeros((3 * groups, slots), F32)
        for g in range(groups):
            left_g = jnp.where(group_row == g, left, 0.0).astype(BF16)
            right_g = jnp.where(group_row == g, right, 0.0).astype(BF16)
            to_res = to_res + dot_nt(left_g, hi_ref[g]) + dot_nt(left_g, lo_ref[g])
            to_list = to_list + dot_nn(right_g, hi_ref[g]) + dot_nn(right_g, lo_ref[g])
        gather = lambda y: y[:groups] + y[groups : 2 * groups] + y[2 * groups :]
        return rise_res * gather(to_res), fold(rise_work * gather(to_list))

    ones = jnp.ones((groups, tracts), F32)
    total_res, total_work = across(ones, ones)
    diag = (total_res + RIDGE, total_work + RIDGE)
    resid = (target_res - total_res, target_work - total_work)

    def apply(v):
        far = across(v[0], fetch(v[1]))
        return tuple(d * x + y for d, x, y in zip(diag, v, far))

    def dot(a, b):
        return total(a[0] * b[0] + a[1] * b[1])

    def unit(w):
        square = dot(w, w)
        some = square > 0.0
        scale = jnp.where(some, lax.rsqrt(jnp.where(some, square, 1.0)), 0.0)
        return square * scale, tuple(x * scale for x in w)

    size, v = unit(resid)
    basis, entries = [v], [size]
    last, off = None, None
    for _ in range(ITERS):
        w = apply(v)
        along = dot(v, w)
        w = tuple(x - along * y for x, y in zip(w, v))
        if last is not None:
            w = tuple(x - off * y for x, y in zip(w, last))
        last = v
        off, v = unit(w)
        entries += [along, off]
        basis.append(v)

    def put(row, value):
        for r in range(reps):
            out_ref[pl.ds(r * sent_rows + row, groups, stride=reps * sent_rows), :] = value

    row = 0
    for v in basis:
        for part in (v[0], swap_blocks(v[1])):
            for at in range(0, tracts, LANES):
                put(row, part[:, at : at + LANES])
                row += 1
    lane = lax.broadcasted_iota(jnp.int32, (groups, LANES), 1)
    numbers = jnp.zeros((groups, LANES), F32)
    for k, entry in enumerate(entries):
        numbers = jnp.where(lane == k, entry, numbers)
    put(row, numbers)
    most = group_rows(at_most, 0)
    for r in range(1, reps):
        most = jnp.maximum(most, group_rows(at_most, r))
    flag_ref[...] = jnp.max(most, axis=0, keepdims=True)


def join_kernel(dims, in_ref, step_res_ref, step_work_ref, resid_res_ref, resid_work_ref):
    devices, sent_rows, tracts, cells = dims["devices"], dims["sent_rows"], dims["tracts"], dims["cells"]

    def take(row):
        return in_ref[pl.ds(row, devices, stride=sent_rows), :]

    numbers = take(sent_rows - 1)
    entry = lambda k: jnp.broadcast_to(numbers[:, k : k + 1], (devices, LANES))
    along = [entry(1 + 2 * k) for k in range(ITERS)]
    off = [entry(2 + 2 * k) for k in range(ITERS)]

    def inner(a, b):
        return jnp.sum(sum(x * y for x, y in zip(a, b)), axis=0, keepdims=True)

    resid = [entry(0)]
    direct = [entry(0)]
    step = []
    norm = inner(resid, resid)
    for turn in range(ITERS):
        image = []
        for k in range(turn + 2):
            value = None
            for term in ((off[k - 1], k - 1), (along[k] if k < ITERS else None, k), (off[k] if k < ITERS else None, k + 1)):
                if 0 <= term[1] <= turn:
                    product = term[0] * direct[term[1]]
                    value = product if value is None else value + product
            image.append(value)
        alpha = norm / inner(direct, image)
        step = [s + alpha * d for s, d in zip(step, direct)] + [alpha * d for d in direct[len(step) :]]
        resid = [r - alpha * i for r, i in zip(resid, image)] + [-alpha * i for i in image[len(resid) :]]
        following = inner(resid, resid)
        beta = following / norm
        direct = [r + beta * d for r, d in zip(resid, direct)] + resid[len(direct) :]
        norm = following

    half = tracts // LANES
    for part, (step_ref, resid_ref) in enumerate(((step_res_ref, resid_res_ref), (step_work_ref, resid_work_ref))):
        for at in range(half):
            vectors = [take((2 * k + part) * half + at) for k in range(ITERS + 1)]
            lanes = slice(at * LANES, (at + 1) * LANES)
            step_ref[:, lanes] = sum(s * v for s, v in zip(step, vectors))[:cells]
            resid_ref[:, lanes] = sum(r * v for r, v in zip(resid, vectors))[:cells]


def round_up(value, unit):
    return -(-value // unit) * unit


def plan_dims(mesh_shape, shapes):
    groups, reps = mesh_shape["geo"], mesh_shape["rep"]
    cells, tracts = shapes["lam"]
    listed = shapes["needed"][1] * shapes["needed"][2]
    slots = listed * BLK
    jobs = shapes["jobs"]
    cap = round_up(max(1, 3 * jobs // (2 * cells)), LANES)
    rows = round_up(3 * cap // LANES + slots // LANES + 1 + tracts // LANES, 8)
    fits = (
        groups * reps >= cells
        and reps == 4
        and groups == 8
        and listed == groups
        and slots == tracts
        and tracts % LANES == 0
        and tracts <= 256
        and jobs % 256 == 0
        and groups * tracts * slots * 4 <= TABLE_BYTES
    )
    return fits, dict(
        devices=groups * reps,
        groups=groups,
        reps=reps,
        cells=cells,
        tracts=tracts,
        slots=slots,
        listed=listed,
        cap=cap,
        rows=rows,
        sent_rows=2 * (ITERS + 1) * (tracts // LANES) + 1,
    )


def owner_plan(dims, base, job_res, job_slot, job_cell, needed, lam_res, lam_work, target_res, target_work):
    devices, rows, sent_rows, cells, tracts = (dims[k] for k in ("devices", "rows", "sent_rows", "cells", "tracts"))
    vmem = pl.BlockSpec(memory_space=pltpu.VMEM)
    smem = pl.BlockSpec(memory_space=pltpu.SMEM)
    flat = lambda x: x.reshape(1, -1)
    packed = pl.pallas_call(
        functools.partial(pack_kernel, dims),
        out_shape=jax.ShapeDtypeStruct((devices * rows, LANES), F32),
        in_specs=[smem] + [vmem] * 8,
        out_specs=vmem,
        name="pack",
    )(needed.reshape(-1), flat(base), flat(job_res), flat(job_slot), flat(job_cell), lam_res, lam_work, target_res, target_work)
    arrived = lax.all_to_all(packed.reshape(devices, rows, LANES), ALL, split_axis=0, concat_axis=0, tiled=True)
    sent, most = pl.pallas_call(
        functools.partial(cell_kernel, dims),
        out_shape=(
            jax.ShapeDtypeStruct((devices * sent_rows, LANES), F32),
            jax.ShapeDtypeStruct((1, LANES), F32),
        ),
        in_specs=[vmem],
        out_specs=(vmem, vmem),
        scratch_shapes=[pltpu.VMEM((dims["groups"], tracts, dims["slots"]), BF16)] * 2,
        name="cell",
    )(arrived.reshape(devices * rows, LANES))
    back = lax.all_to_all(sent.reshape(devices, sent_rows, 1, LANES), ALL, split_axis=0, concat_axis=0, tiled=True)
    outs = pl.pallas_call(
        functools.partial(join_kernel, dims),
        out_shape=(jax.ShapeDtypeStruct((cells, tracts), F32),) * 4,
        in_specs=[vmem],
        out_specs=(vmem,) * 4,
        name="join",
    )(back.reshape(devices * sent_rows, LANES))
    return outs, most[0, 0] > dims["cap"]


def body(mesh_shape, *args):
    base, needed, lam_res = args[0], args[4], args[5]
    fits, dims = plan_dims(mesh_shape, {"lam": lam_res.shape, "needed": needed.shape, "jobs": base.shape[0]})
    if not fits:
        return start_plan(*args)
    outs, over = owner_plan(dims, *args)
    return lax.cond(over, lambda: tuple(start_plan(*args)), lambda: tuple(outs))


def solution(mesh):
    in_specs = (P(ALL),) * 4 + (P("geo", None, None),) + (P(None, "geo"),) * 4
    out_specs = (P(None, "geo"),) * 4
    return jax.shard_map(
        functools.partial(body, dict(mesh.shape)), mesh=mesh, in_specs=in_specs, out_specs=out_specs, check_vma=False
    )
```

```python
import functools

import jax
import jax.numpy as jnp
from jax import lax
from jax.experimental import pallas as pl
from jax.experimental.pallas import tpu as pltpu
from jax.sharding import PartitionSpec as P

BLK = 32
ITERS = 3
RIDGE = 0.5
LANES = 128
ALL = ("geo", "rep")

F32 = jnp.float32
BF16 = jnp.bfloat16


def start_plan(base, job_res, job_slot, job_cell, needed, lam_res, lam_work, target_res, target_work):
    cells, tracts_dev = lam_res.shape
    blocks_dev = tracts_dev // BLK
    requests = lax.all_to_all(needed[0], "geo", split_axis=0, concat_axis=0, tiled=True)
    sources, listed = requests.shape
    onehot = (
        requests[:, :, None] == jnp.arange(blocks_dev, dtype=jnp.int32)[None, None, :]
    ).astype(jnp.float32)
    slot_shape = (sources, listed, cells, BLK)
    slot_count = sources * listed * cells * BLK
    res_index = job_cell * tracts_dev + job_res
    work_index = (job_slot // BLK * cells + job_cell) * BLK + job_slot % BLK

    def serve(table):
        blocks = table.reshape(cells, blocks_dev, BLK).transpose(1, 0, 2)
        return jnp.take(blocks, requests, axis=0)

    def pick(fetched):
        return fetched.reshape(-1)[work_index]

    def fold(arrived):
        return jnp.einsum("skb,skcx->cbx", onehot, arrived, precision=lax.Precision.HIGHEST)

    def totals(values):
        res_part = jax.ops.segment_sum(values, res_index, num_segments=cells * tracts_dev).reshape(
            cells, tracts_dev
        )
        work_part = jax.ops.segment_sum(values, work_index, num_segments=slot_count).reshape(
            slot_shape
        )
        arrived = lax.all_to_all(work_part, "geo", split_axis=0, concat_axis=0, tiled=True)
        folded = fold(arrived)
        return lax.psum((res_part, folded.reshape(cells, tracts_dev)), "rep")

    def inner(a_res, a_work, b_res, b_work):
        return lax.psum(jnp.sum(a_res * b_res) + jnp.sum(a_work * b_work), "geo")

    fetched_lam = lax.all_to_all(serve(lam_work), "geo", split_axis=0, concat_axis=0, tiled=True)
    weight = base * jnp.exp(lam_res.reshape(-1)[res_index] + pick(fetched_lam))
    total_res, total_work = totals(weight)
    resid_res = -(total_res - target_res)
    resid_work = -(total_work - target_work)
    norm = inner(resid_res, resid_work, resid_res, resid_work)
    zeros = jnp.zeros_like(resid_res)

    def turn(_, state):
        step_res, step_work, resid_res, resid_work, dir_res, dir_work, norm_now = state
        dir_piece = lax.all_to_all(serve(dir_work), "geo", split_axis=0, concat_axis=0, tiled=True)
        along = dir_res.reshape(-1)[res_index] + pick(dir_piece)
        image_res, image_work = totals(weight * along)
        image_res = image_res + RIDGE * dir_res
        image_work = image_work + RIDGE * dir_work
        alpha = norm_now / inner(dir_res, dir_work, image_res, image_work)
        step_res = step_res + alpha * dir_res
        step_work = step_work + alpha * dir_work
        resid_res = resid_res - alpha * image_res
        resid_work = resid_work - alpha * image_work
        norm_next = inner(resid_res, resid_work, resid_res, resid_work)
        dir_res = resid_res + norm_next / norm_now * dir_res
        dir_work = resid_work + norm_next / norm_now * dir_work
        return step_res, step_work, resid_res, resid_work, dir_res, dir_work, norm_next

    state = (zeros, zeros, resid_res, resid_work, resid_res, resid_work, norm)
    return lax.fori_loop(0, ITERS, turn, state)[:4]


def split3(x):
    high = x.astype(BF16)
    rest = x - high.astype(F32)
    mid = rest.astype(BF16)
    low = (rest - mid.astype(F32)).astype(BF16)
    return high, mid, low


def dot_nt(a, b):
    return lax.dot_general(a, b, (((1,), (1,)), ((), ())), preferred_element_type=F32)


def dot_nn(a, b):
    return jnp.dot(a, b, preferred_element_type=F32)


def pack_kernel(dims, needed_ref, base_ref, res_ref, slot_ref, cell_ref, a_ref, b_ref, c_ref, d_ref, out_ref):
    devices, rows, cap, listed, cells = dims["devices"], dims["rows"], dims["cap"], dims["listed"], dims["cells"]
    tracts = a_ref.shape[1]
    jobs = cell_ref.shape[1]
    chunk = 256
    cell = cell_ref[...]
    member = lax.broadcasted_iota(jnp.int32, (devices, jobs), 0) == cell
    member_b = member.astype(F32).astype(BF16)
    before = lax.broadcasted_iota(jnp.int32, (chunk, chunk), 0) < lax.broadcasted_iota(jnp.int32, (chunk, chunk), 1)
    before = before.astype(F32).astype(BF16)
    ranks = []
    count = jnp.zeros((devices, 1), F32)
    for at in range(0, jobs, chunk):
        part = member_b[:, at : at + chunk]
        seen = dot_nn(part, before) + count
        own = member[:, at : at + chunk]
        ranks.append(jnp.sum(jnp.where(own, seen, 0.0), axis=0, keepdims=True))
        count = count + jnp.sum(own.astype(F32), axis=1, keepdims=True)
    rank = jnp.concatenate(ranks, axis=1).astype(jnp.int32)
    largest = jnp.max(count, axis=0, keepdims=True)
    chosen = (lax.broadcasted_iota(jnp.int32, (cap, jobs), 0) == rank).astype(F32).astype(BF16)
    values = (res_ref[...].astype(F32), slot_ref[...].astype(F32)) + tuple(x.astype(F32) for x in split3(base_ref[...]))
    held = jnp.concatenate([jnp.where(member, value, 0.0).astype(BF16) for value in values], axis=0)
    moved = dot_nt(held, chosen)
    moved = [moved[k * devices : (k + 1) * devices] for k in range(len(values))]
    sent = (moved[0], moved[1], moved[2] + moved[3] + moved[4])

    def put(row, value):
        out_ref[pl.ds(row, devices, stride=rows), :] = value

    row = 0
    for value in sent:
        put(row, value)
        row += 1
    rep = lax.axis_index("rep")
    mine = a_ref[...]
    for k, ref in enumerate((b_ref, c_ref, d_ref)):
        mine = jnp.where(rep == k + 1, ref[...], mine)
    mine = jnp.concatenate([mine, jnp.zeros((devices - cells, tracts), F32)], axis=0)
    for at in range(0, tracts, LANES):
        put(row, mine[:, at : at + LANES])
        row += 1
    owner = lax.broadcasted_iota(jnp.int32, (devices, listed * BLK), 1) // BLK
    wanted = jnp.zeros((devices, listed * BLK), F32)
    for p in range(listed):
        wanted = jnp.where(owner == p, needed_ref[p].astype(F32), wanted)
    for at in range(0, listed * BLK, LANES):
        put(row, wanted[:, at : at + LANES])
        row += 1
    put(row, jnp.broadcast_to(largest, (devices, LANES)))


def cell_kernel(dims, in_ref, out_ref, flag_ref, pick_ref, mask_ref, weight_ref, hot_ref, turn_ref):
    rows, groups, reps, sent_rows = (dims[k] for k in ("rows", "groups", "reps", "sent_rows"))
    at_res, at_slot, at_base, at_own, at_need, at_most = 0, 1, 2, 3, 5, 7
    tile = (groups, LANES)
    sub = lax.broadcasted_iota(jnp.int32, tile, 0)
    segment = lax.broadcasted_iota(jnp.int32, tile, 1) // BLK

    side = LANES // BLK

    def row_of(row, device):
        return jnp.broadcast_to(in_ref[pl.ds(device * rows + row, 1), :], tile)

    def shifted(x, segments):
        return pltpu.roll(x, BLK * (segments % side), 1) if segments % side else x

    def unfold(row, rep, place):
        tiles = []
        for half in range(groups // side):
            x = in_ref[pl.ds(rep * rows + row + half, groups, stride=reps * rows), :]
            tiles += [shifted(x, place - k) for k in range(side)]
        return tiles

    def turned(tiles, slot):
        for b, x in enumerate(tiles):
            turn_ref[slot, pl.ds(b, groups, stride=groups), :] = x
        return [turn_ref[slot, pl.ds(g * groups, groups), :] for g in range(groups)]

    def both(res_rep, work_rep, slot):
        res, work = turned(unfold(at_own, res_rep, 0), slot), unfold(at_own, work_rep, 1)
        return [jnp.where(segment == 0, x, jnp.where(segment == 1, y, 0.0)) for x, y in zip(res, work)]

    need = [jnp.where(segment == 1, x, -1.0) for x in turned(unfold(at_need, 0, 1), 0)]

    def fetch(v):
        tables = []
        for g in range(groups):
            table = jnp.where(segment == 0, v[g], 0.0)
            for b in range(groups):
                table = jnp.where(need[g] == float(b), v[b], table)
            tables.append(table)
        return tables

    low = lax.broadcasted_iota(jnp.int32, (BLK, LANES), 0)
    for g in range(groups):
        for r in range(reps):
            device = g * reps + r
            res = row_of(at_res, device).astype(jnp.int32)
            slot = row_of(at_slot, device).astype(jnp.int32)
            pick_ref[device, :groups, :] = res % BLK
            pick_ref[device, groups:, :] = slot % BLK + BLK
            mask_ref[device, :groups, :] = (res // BLK == sub).astype(F32)
            mask_ref[device, groups:, :] = (slot // BLK == sub).astype(F32)
            lanes = slice(r * LANES, (r + 1) * LANES)
            hot_ref[g, :BLK, lanes] = (low == (res % BLK)[:1]).astype(F32).astype(BF16)
            hot_ref[g, BLK:, lanes] = (low == (slot % BLK)[:1]).astype(F32).astype(BF16)

    def along(device, table):
        picked = jnp.take_along_axis(table, pick_ref[device, :groups, :], axis=1) * mask_ref[device, :groups, :]
        picked += jnp.take_along_axis(table, pick_ref[device, groups:, :], axis=1) * mask_ref[device, groups:, :]
        return jnp.broadcast_to(jnp.sum(picked, axis=0, keepdims=True), tile)

    empty = jnp.zeros((2 * groups, LANES - 2 * BLK), F32)

    def scatter(values):
        res, folded = [], [jnp.zeros(tile, F32)] * groups
        for g in range(groups):
            columns = []
            for r in range(reps):
                device = g * reps + r
                mask = mask_ref[device]
                parts = [jnp.concatenate([x.astype(F32)] * 2, axis=0) * mask for x in split3(values[device])]
                columns.append(jnp.concatenate(parts, axis=0).astype(BF16))
            sums = dot_nt(jnp.concatenate(columns, axis=1), hot_ref[g])
            sums = sums[: 2 * groups] + sums[2 * groups : 4 * groups] + sums[4 * groups :]
            sums = jnp.concatenate([sums, empty], axis=1)
            res.append(jnp.where(segment == 0, sums[:groups], 0.0))
            for b in range(groups):
                folded[b] = folded[b] + jnp.where(need[g] == float(b), sums[groups:], 0.0)
        return [x + y for x, y in zip(res, folded)]

    lam = fetch(both(0, 1, 1))
    weights = []
    for device in range(groups * reps):
        weight = row_of(at_base, device) * jnp.exp(along(device, lam[device // reps]))
        weight_ref[device] = weight
        weights.append(weight)
    resid = [x - y for x, y in zip(both(2, 3, 2), scatter(weights))]

    def apply(v):
        tables = fetch(v)
        image = scatter([weight_ref[device] * along(device, tables[device // reps]) for device in range(groups * reps)])
        return [x + RIDGE * y for x, y in zip(image, v)]

    def dot(a, b):
        products = [x * y for x, y in zip(a, b)]
        while len(products) > 1:
            products = [x + y for x, y in zip(products[::2], products[1::2])]
        return jnp.sum(jnp.sum(products[0], axis=0, keepdims=True), axis=1, keepdims=True)

    def unit(w):
        square = dot(w, w)
        some = square > 0.0
        scale = jnp.where(some, lax.rsqrt(jnp.where(some, square, 1.0)), 0.0)
        return square * scale, [x * scale for x in w]

    size, v = unit(resid)
    basis, entries = [v], [size]
    last, off = None, None
    for _ in range(ITERS):
        w = apply(v)
        if last is not None:
            w = [x - off * y for x, y in zip(w, last)]
        middle = dot(v, w)
        w = [x - middle * y for x, y in zip(w, v)]
        last = v
        off, v = unit(w)
        entries += [middle, off]
        basis.append(v)

    def put(row, value):
        for r in range(reps):
            out_ref[pl.ds(r * sent_rows + row, groups, stride=reps * sent_rows), :] = value

    for k, v in enumerate(basis):
        for part, tiles in enumerate((turned(v, 3 + k), v)):
            for half in range(groups // side):
                row = jnp.zeros(tile, F32)
                for q in range(side):
                    row = jnp.where(segment == q, shifted(tiles[half * side + q], q - part), row)
                put((2 * k + part) * (groups // side) + half, row)
    lane = lax.broadcasted_iota(jnp.int32, tile, 1)
    numbers = jnp.zeros(tile, F32)
    for k, entry in enumerate(entries):
        numbers = jnp.where(lane == k, entry, numbers)
    put(sent_rows - 1, numbers)
    most = in_ref[pl.ds(at_most, groups * reps, stride=rows), :]
    flag_ref[...] = jnp.max(most, axis=0, keepdims=True)


def join_kernel(dims, in_ref, step_res_ref, step_work_ref, resid_res_ref, resid_work_ref):
    devices, sent_rows, groups, cells = dims["devices"], dims["sent_rows"], dims["groups"], dims["cells"]
    tile = (devices, LANES)

    def take(row):
        return in_ref[pl.ds(row, devices, stride=sent_rows), :]

    numbers = take(sent_rows - 1)
    entry = lambda k: jnp.broadcast_to(numbers[:, k : k + 1], tile)
    along = [entry(1 + 2 * k) for k in range(ITERS)]
    off = [entry(2 + 2 * k) for k in range(ITERS)]

    def inner(a, b):
        return jnp.sum(sum(x * y for x, y in zip(a, b)), axis=0, keepdims=True)

    resid = [entry(0)]
    direct = [entry(0)]
    step = []
    norm = inner(resid, resid)
    for turn in range(ITERS):
        image = []
        for k in range(turn + 2):
            value = None
            for term in ((off[k - 1], k - 1), (along[k] if k < ITERS else None, k), (off[k] if k < ITERS else None, k + 1)):
                if 0 <= term[1] <= turn:
                    product = term[0] * direct[term[1]]
                    value = product if value is None else value + product
            image.append(value)
        alpha = norm / inner(direct, image)
        step = [s + alpha * d for s, d in zip(step, direct)] + [alpha * d for d in direct[len(step) :]]
        resid = [r - alpha * i for r, i in zip(resid, image)] + [-alpha * i for i in image[len(resid) :]]
        following = inner(resid, resid)
        beta = following / norm
        direct = [r + beta * d for r, d in zip(resid, direct)] + resid[len(direct) :]
        norm = following

    half = groups * BLK // LANES
    for part, (step_ref, resid_ref) in enumerate(((step_res_ref, resid_res_ref), (step_work_ref, resid_work_ref))):
        for at in range(half):
            vectors = [take((2 * k + part) * half + at) for k in range(ITERS + 1)]
            lanes = slice(at * LANES, (at + 1) * LANES)
            step_ref[:, lanes] = sum(s * v for s, v in zip(step, vectors))[:cells]
            resid_ref[:, lanes] = sum(r * v for r, v in zip(resid, vectors))[:cells]


def round_up(value, unit):
    return -(-value // unit) * unit


def plan_dims(mesh_shape, shapes):
    groups, reps = mesh_shape["geo"], mesh_shape["rep"]
    cells, tracts = shapes["lam"]
    listed = shapes["needed"][1] * shapes["needed"][2]
    slots = listed * BLK
    jobs = shapes["jobs"]
    cap = round_up(max(1, 3 * jobs // (2 * cells)), LANES)
    rows = 8
    fits = (
        groups * reps >= cells
        and reps == 4
        and groups == 8
        and listed == groups
        and tracts == groups * BLK
        and cap == LANES
        and jobs % 256 == 0
    )
    return fits, dict(
        devices=groups * reps,
        groups=groups,
        reps=reps,
        cells=cells,
        tracts=tracts,
        listed=listed,
        cap=cap,
        rows=rows,
        sent_rows=2 * groups + 1,
    )


def owner_plan(dims, base, job_res, job_slot, job_cell, needed, lam_res, lam_work, target_res, target_work):
    devices, rows, sent_rows, cells, tracts, groups, reps = (
        dims[k] for k in ("devices", "rows", "sent_rows", "cells", "tracts", "groups", "reps")
    )
    vmem = pl.BlockSpec(memory_space=pltpu.VMEM)
    smem = pl.BlockSpec(memory_space=pltpu.SMEM)
    flat = lambda x: x.reshape(1, -1)
    packed = pl.pallas_call(
        functools.partial(pack_kernel, dims),
        out_shape=jax.ShapeDtypeStruct((devices * rows, LANES), F32),
        in_specs=[smem] + [vmem] * 8,
        out_specs=vmem,
        name="pack",
    )(needed.reshape(-1), flat(base), flat(job_res), flat(job_slot), flat(job_cell), lam_res, lam_work, target_res, target_work)
    arrived = lax.all_to_all(packed.reshape(devices, rows, LANES), ALL, split_axis=0, concat_axis=0, tiled=True)
    sent, most = pl.pallas_call(
        functools.partial(cell_kernel, dims),
        out_shape=(
            jax.ShapeDtypeStruct((devices * sent_rows, LANES), F32),
            jax.ShapeDtypeStruct((1, LANES), F32),
        ),
        in_specs=[vmem],
        out_specs=(vmem, vmem),
        scratch_shapes=[
            pltpu.VMEM((devices, 2 * groups, LANES), jnp.int32),
            pltpu.VMEM((devices, 2 * groups, LANES), F32),
            pltpu.VMEM((devices, groups, LANES), F32),
            pltpu.VMEM((groups, 2 * BLK, reps * LANES), BF16),
            pltpu.VMEM((3 + ITERS + 1, groups * groups, LANES), F32),
        ],
        name="cell",
    )(arrived.reshape(devices * rows, LANES))
    back = lax.all_to_all(sent.reshape(devices, sent_rows, 1, LANES), ALL, split_axis=0, concat_axis=0, tiled=True)
    outs = pl.pallas_call(
        functools.partial(join_kernel, dims),
        out_shape=(jax.ShapeDtypeStruct((cells, tracts), F32),) * 4,
        in_specs=[vmem],
        out_specs=(vmem,) * 4,
        name="join",
    )(back.reshape(devices * sent_rows, LANES))
    return outs, most[0, 0] > dims["cap"]


def body(mesh_shape, *args):
    base, needed, lam_res = args[0], args[4], args[5]
    fits, dims = plan_dims(mesh_shape, {"lam": lam_res.shape, "needed": needed.shape, "jobs": base.shape[0]})
    if not fits:
        return start_plan(*args)
    outs, over = owner_plan(dims, *args)
    return lax.cond(over, lambda: tuple(start_plan(*args)), lambda: tuple(outs))


def solution(mesh):
    in_specs = (P(ALL),) * 4 + (P("geo", None, None),) + (P(None, "geo"),) * 4
    out_specs = (P(None, "geo"),) * 4
    return jax.shard_map(
        functools.partial(body, dict(mesh.shape)), mesh=mesh, in_specs=in_specs, out_specs=out_specs, check_vma=False
    )
```

```python
import functools

import jax
import jax.numpy as jnp
from jax import lax
from jax.experimental import pallas as pl
from jax.experimental.pallas import tpu as pltpu
from jax.sharding import PartitionSpec as P

BLK = 32
ITERS = 3
RIDGE = 0.5
LANES = 128
ALL = ("geo", "rep")

F32 = jnp.float32
BF16 = jnp.bfloat16


def start_plan(base, job_res, job_slot, job_cell, needed, lam_res, lam_work, target_res, target_work):
    cells, tracts_dev = lam_res.shape
    blocks_dev = tracts_dev // BLK
    requests = lax.all_to_all(needed[0], "geo", split_axis=0, concat_axis=0, tiled=True)
    sources, listed = requests.shape
    onehot = (
        requests[:, :, None] == jnp.arange(blocks_dev, dtype=jnp.int32)[None, None, :]
    ).astype(jnp.float32)
    slot_shape = (sources, listed, cells, BLK)
    slot_count = sources * listed * cells * BLK
    res_index = job_cell * tracts_dev + job_res
    work_index = (job_slot // BLK * cells + job_cell) * BLK + job_slot % BLK

    def serve(table):
        blocks = table.reshape(cells, blocks_dev, BLK).transpose(1, 0, 2)
        return jnp.take(blocks, requests, axis=0)

    def pick(fetched):
        return fetched.reshape(-1)[work_index]

    def fold(arrived):
        return jnp.einsum("skb,skcx->cbx", onehot, arrived, precision=lax.Precision.HIGHEST)

    def totals(values):
        res_part = jax.ops.segment_sum(values, res_index, num_segments=cells * tracts_dev).reshape(
            cells, tracts_dev
        )
        work_part = jax.ops.segment_sum(values, work_index, num_segments=slot_count).reshape(
            slot_shape
        )
        arrived = lax.all_to_all(work_part, "geo", split_axis=0, concat_axis=0, tiled=True)
        folded = fold(arrived)
        return lax.psum((res_part, folded.reshape(cells, tracts_dev)), "rep")

    def inner(a_res, a_work, b_res, b_work):
        return lax.psum(jnp.sum(a_res * b_res) + jnp.sum(a_work * b_work), "geo")

    fetched_lam = lax.all_to_all(serve(lam_work), "geo", split_axis=0, concat_axis=0, tiled=True)
    weight = base * jnp.exp(lam_res.reshape(-1)[res_index] + pick(fetched_lam))
    total_res, total_work = totals(weight)
    resid_res = -(total_res - target_res)
    resid_work = -(total_work - target_work)
    norm = inner(resid_res, resid_work, resid_res, resid_work)
    zeros = jnp.zeros_like(resid_res)

    def turn(_, state):
        step_res, step_work, resid_res, resid_work, dir_res, dir_work, norm_now = state
        dir_piece = lax.all_to_all(serve(dir_work), "geo", split_axis=0, concat_axis=0, tiled=True)
        along = dir_res.reshape(-1)[res_index] + pick(dir_piece)
        image_res, image_work = totals(weight * along)
        image_res = image_res + RIDGE * dir_res
        image_work = image_work + RIDGE * dir_work
        alpha = norm_now / inner(dir_res, dir_work, image_res, image_work)
        step_res = step_res + alpha * dir_res
        step_work = step_work + alpha * dir_work
        resid_res = resid_res - alpha * image_res
        resid_work = resid_work - alpha * image_work
        norm_next = inner(resid_res, resid_work, resid_res, resid_work)
        dir_res = resid_res + norm_next / norm_now * dir_res
        dir_work = resid_work + norm_next / norm_now * dir_work
        return step_res, step_work, resid_res, resid_work, dir_res, dir_work, norm_next

    state = (zeros, zeros, resid_res, resid_work, resid_res, resid_work, norm)
    return lax.fori_loop(0, ITERS, turn, state)[:4]


def split3(x):
    high = x.astype(BF16)
    rest = x - high.astype(F32)
    mid = rest.astype(BF16)
    low = (rest - mid.astype(F32)).astype(BF16)
    return high, mid, low


def dot_nt(a, b):
    return lax.dot_general(a, b, (((1,), (1,)), ((), ())), preferred_element_type=F32)


def dot_nn(a, b):
    return jnp.dot(a, b, preferred_element_type=F32)


def pack_kernel(dims, needed_ref, base_ref, res_ref, slot_ref, cell_ref, a_ref, b_ref, c_ref, d_ref, out_ref):
    devices, rows, cap, listed, cells = dims["devices"], dims["rows"], dims["cap"], dims["listed"], dims["cells"]
    tracts = a_ref.shape[1]
    jobs = cell_ref.shape[1]
    chunk = 256
    cell = cell_ref[...]
    member = lax.broadcasted_iota(jnp.int32, (devices, jobs), 0) == cell
    member_b = member.astype(F32).astype(BF16)
    before = lax.broadcasted_iota(jnp.int32, (chunk, chunk), 0) < lax.broadcasted_iota(jnp.int32, (chunk, chunk), 1)
    before = before.astype(F32).astype(BF16)
    ranks = []
    count = jnp.zeros((devices, 1), F32)
    for at in range(0, jobs, chunk):
        part = member_b[:, at : at + chunk]
        seen = dot_nn(part, before) + count
        own = member[:, at : at + chunk]
        ranks.append(jnp.sum(jnp.where(own, seen, 0.0), axis=0, keepdims=True))
        count = count + jnp.sum(own.astype(F32), axis=1, keepdims=True)
    rank = jnp.concatenate(ranks, axis=1).astype(jnp.int32)
    largest = jnp.max(count, axis=0, keepdims=True)
    chosen = (lax.broadcasted_iota(jnp.int32, (cap, jobs), 0) == rank).astype(F32).astype(BF16)
    values = (res_ref[...].astype(F32), slot_ref[...].astype(F32)) + tuple(x.astype(F32) for x in split3(base_ref[...]))
    held = jnp.concatenate([jnp.where(member, value, 0.0).astype(BF16) for value in values], axis=0)
    moved = dot_nt(held, chosen)
    moved = [moved[k * devices : (k + 1) * devices] for k in range(len(values))]
    sent = (moved[0], moved[1], moved[2] + moved[3] + moved[4])

    def put(row, value):
        out_ref[pl.ds(row, devices, stride=rows), :] = value

    row = 0
    for value in sent:
        put(row, value)
        row += 1
    rep = lax.axis_index("rep")
    mine = a_ref[...]
    for k, ref in enumerate((b_ref, c_ref, d_ref)):
        mine = jnp.where(rep == k + 1, ref[...], mine)
    mine = jnp.concatenate([mine, jnp.zeros((devices - cells, tracts), F32)], axis=0)
    for at in range(0, tracts, LANES):
        put(row, mine[:, at : at + LANES])
        row += 1
    lane = lax.broadcasted_iota(jnp.int32, (devices, LANES), 1)
    head = jnp.broadcast_to(largest, (devices, LANES))
    for p in range(listed):
        head = jnp.where(lane == p, needed_ref[p].astype(F32), head)
    put(row, head)


def cell_kernel(dims, in_ref, out_ref, flag_ref, pick_ref, mask_ref, weight_ref, hot_ref, turn_ref):
    rows, groups, reps, sent_rows = (dims[k] for k in ("rows", "groups", "reps", "sent_rows"))
    at_res, at_slot, at_base, at_own, at_head = 0, 1, 2, 3, 5
    tile = (groups, LANES)
    sub = lax.broadcasted_iota(jnp.int32, tile, 0)
    segment = lax.broadcasted_iota(jnp.int32, tile, 1) // BLK

    side = LANES // BLK

    def row_of(row, device):
        return jnp.broadcast_to(in_ref[pl.ds(device * rows + row, 1), :], tile)

    def shifted(x, segments):
        return pltpu.roll(x, BLK * (segments % side), 1) if segments % side else x

    def unfold(row, rep, place):
        tiles = []
        for half in range(groups // side):
            x = in_ref[pl.ds(rep * rows + row + half, groups, stride=reps * rows), :]
            tiles += [shifted(x, place - k) for k in range(side)]
        return tiles

    def turned(tiles, slot):
        for b, x in enumerate(tiles):
            turn_ref[slot, pl.ds(b, groups, stride=groups), :] = x
        return [turn_ref[slot, pl.ds(g * groups, groups), :] for g in range(groups)]

    def both(res_rep, work_rep, slot):
        res, work = turned(unfold(at_own, res_rep, 0), slot), unfold(at_own, work_rep, 1)
        return [jnp.where(segment == 0, x, jnp.where(segment == 1, y, 0.0)) for x, y in zip(res, work)]

    lane = lax.broadcasted_iota(jnp.int32, tile, 1)
    need = []
    for g in range(groups):
        own = jnp.sum(jnp.where(lane == sub, row_of(at_head, g * reps), 0.0), axis=1, keepdims=True)
        need.append(jnp.where(segment == 1, own, -1.0))

    def fetch(v):
        tables = []
        for g in range(groups):
            table = jnp.where(segment == 0, v[g], 0.0)
            for b in range(groups):
                table = jnp.where(need[g] == float(b), v[b], table)
            tables.append(table)
        return tables

    low = lax.broadcasted_iota(jnp.int32, (BLK, LANES), 0)
    for g in range(groups):
        for r in range(reps):
            device = g * reps + r
            res = row_of(at_res, device).astype(jnp.int32)
            slot = row_of(at_slot, device).astype(jnp.int32)
            pick_ref[device, :groups, :] = res % BLK
            pick_ref[device, groups:, :] = slot % BLK + BLK
            mask_ref[device, :groups, :] = (res // BLK == sub).astype(F32)
            mask_ref[device, groups:, :] = (slot // BLK == sub).astype(F32)
            lanes = slice(r * LANES, (r + 1) * LANES)
            hot_ref[g, :BLK, lanes] = (low == (res % BLK)[:1]).astype(F32).astype(BF16)
            hot_ref[g, BLK:, lanes] = (low == (slot % BLK)[:1]).astype(F32).astype(BF16)

    def along(device, table):
        picked = jnp.take_along_axis(table, pick_ref[device, :groups, :], axis=1) * mask_ref[device, :groups, :]
        picked += jnp.take_along_axis(table, pick_ref[device, groups:, :], axis=1) * mask_ref[device, groups:, :]
        return jnp.broadcast_to(jnp.sum(picked, axis=0, keepdims=True), tile)

    empty = jnp.zeros((2 * groups, LANES - 2 * BLK), F32)

    def scatter(values):
        res, folded = [], [jnp.zeros(tile, F32)] * groups
        for g in range(groups):
            columns = []
            for r in range(reps):
                device = g * reps + r
                mask = mask_ref[device].astype(BF16)
                columns.append(jnp.concatenate([jnp.concatenate([x] * 2, axis=0) * mask for x in split3(values[device])], axis=0))
            sums = dot_nt(jnp.concatenate(columns, axis=1), hot_ref[g])
            sums = sums[: 2 * groups] + sums[2 * groups : 4 * groups] + sums[4 * groups :]
            sums = jnp.concatenate([sums, empty], axis=1)
            res.append(jnp.where(segment == 0, sums[:groups], 0.0))
            for b in range(groups):
                folded[b] = folded[b] + jnp.where(need[g] == float(b), sums[groups:], 0.0)
        return [x + y for x, y in zip(res, folded)]

    lam = fetch(both(0, 1, 0))
    weights = []
    for device in range(groups * reps):
        weight = row_of(at_base, device) * jnp.exp(along(device, lam[device // reps]))
        weight_ref[device] = weight
        weights.append(weight)
    resid = [x - y for x, y in zip(both(2, 3, 1), scatter(weights))]

    def apply(v):
        tables = fetch(v)
        image = scatter([weight_ref[device] * along(device, tables[device // reps]) for device in range(groups * reps)])
        return [x + RIDGE * y for x, y in zip(image, v)]

    def dot(a, b):
        products = [x * y for x, y in zip(a, b)]
        while len(products) > 1:
            products = [x + y for x, y in zip(products[::2], products[1::2])]
        return jnp.sum(jnp.sum(products[0], axis=0, keepdims=True), axis=1, keepdims=True)

    def unit(w):
        square = dot(w, w)
        some = square > 0.0
        scale = jnp.where(some, lax.rsqrt(jnp.where(some, square, 1.0)), 0.0)
        return square * scale, [x * scale for x in w]

    size, v = unit(resid)
    basis, entries = [v], [size]
    last, off = None, None
    for _ in range(ITERS):
        w = apply(v)
        if last is not None:
            w = [x - off * y for x, y in zip(w, last)]
        middle = dot(v, w)
        w = [x - middle * y for x, y in zip(w, v)]
        last = v
        off, v = unit(w)
        entries += [middle, off]
        basis.append(v)

    def put(row, value):
        for r in range(reps):
            out_ref[pl.ds(r * sent_rows + row, groups, stride=reps * sent_rows), :] = value

    for k, v in enumerate(basis):
        for part, tiles in enumerate((turned(v, 2 + k), v)):
            for half in range(groups // side):
                row = jnp.zeros(tile, F32)
                for q in range(side):
                    row = jnp.where(segment == q, shifted(tiles[half * side + q], q - part), row)
                put((2 * k + part) * (groups // side) + half, row)
    numbers = jnp.zeros(tile, F32)
    for k, entry in enumerate(entries):
        numbers = jnp.where(lane == k, entry, numbers)
    put(sent_rows - 1, numbers)
    most = in_ref[pl.ds(at_head, groups * reps, stride=rows), :]
    most = jnp.max(most, axis=0, keepdims=True)
    flag_ref[...] = jnp.broadcast_to(most[:, LANES - 1 :], (1, LANES))


def join_kernel(dims, in_ref, step_res_ref, step_work_ref, resid_res_ref, resid_work_ref):
    devices, sent_rows, groups, cells = dims["devices"], dims["sent_rows"], dims["groups"], dims["cells"]
    tile = (devices, LANES)

    def take(row):
        return in_ref[pl.ds(row, devices, stride=sent_rows), :]

    numbers = take(sent_rows - 1)
    entry = lambda k: jnp.broadcast_to(numbers[:, k : k + 1], tile)
    along = [entry(1 + 2 * k) for k in range(ITERS)]
    off = [entry(2 + 2 * k) for k in range(ITERS)]

    def inner(a, b):
        return jnp.sum(sum(x * y for x, y in zip(a, b)), axis=0, keepdims=True)

    resid = [entry(0)]
    direct = [entry(0)]
    step = []
    norm = inner(resid, resid)
    for turn in range(ITERS):
        image = []
        for k in range(turn + 2):
            value = None
            for term in ((off[k - 1], k - 1), (along[k] if k < ITERS else None, k), (off[k] if k < ITERS else None, k + 1)):
                if 0 <= term[1] <= turn:
                    product = term[0] * direct[term[1]]
                    value = product if value is None else value + product
            image.append(value)
        alpha = norm / inner(direct, image)
        step = [s + alpha * d for s, d in zip(step, direct)] + [alpha * d for d in direct[len(step) :]]
        resid = [r - alpha * i for r, i in zip(resid, image)] + [-alpha * i for i in image[len(resid) :]]
        following = inner(resid, resid)
        beta = following / norm
        direct = [r + beta * d for r, d in zip(resid, direct)] + resid[len(direct) :]
        norm = following

    half = groups * BLK // LANES
    for part, (step_ref, resid_ref) in enumerate(((step_res_ref, resid_res_ref), (step_work_ref, resid_work_ref))):
        for at in range(half):
            vectors = [take((2 * k + part) * half + at) for k in range(ITERS + 1)]
            lanes = slice(at * LANES, (at + 1) * LANES)
            step_ref[:, lanes] = sum(s * v for s, v in zip(step, vectors))[:cells]
            resid_ref[:, lanes] = sum(r * v for r, v in zip(resid, vectors))[:cells]


def round_up(value, unit):
    return -(-value // unit) * unit


def plan_dims(mesh_shape, shapes):
    groups, reps = mesh_shape["geo"], mesh_shape["rep"]
    cells, tracts = shapes["lam"]
    listed = shapes["needed"][1] * shapes["needed"][2]
    slots = listed * BLK
    jobs = shapes["jobs"]
    cap = round_up(max(1, 3 * jobs // (2 * cells)), LANES)
    rows = 6
    fits = (
        groups * reps >= cells
        and reps == 4
        and groups == 8
        and listed == groups
        and tracts == groups * BLK
        and cap == LANES
        and jobs % 256 == 0
    )
    return fits, dict(
        devices=groups * reps,
        groups=groups,
        reps=reps,
        cells=cells,
        tracts=tracts,
        listed=listed,
        cap=cap,
        rows=rows,
        sent_rows=2 * groups + 1,
    )


def owner_plan(dims, base, job_res, job_slot, job_cell, needed, lam_res, lam_work, target_res, target_work):
    devices, rows, sent_rows, cells, tracts, groups, reps = (
        dims[k] for k in ("devices", "rows", "sent_rows", "cells", "tracts", "groups", "reps")
    )
    vmem = pl.BlockSpec(memory_space=pltpu.VMEM)
    smem = pl.BlockSpec(memory_space=pltpu.SMEM)
    flat = lambda x: in_hbm(x.reshape(1, -1))
    in_hbm = lambda x: pltpu.with_memory_space_constraint(x, pltpu.HBM)
    in_vmem = lambda x: pltpu.with_memory_space_constraint(x, pltpu.VMEM)
    packed = pl.pallas_call(
        functools.partial(pack_kernel, dims),
        out_shape=pltpu.VMEM((devices * rows, LANES), F32),
        in_specs=[smem] + [vmem] * 8,
        out_specs=vmem,
        name="pack",
    )(
        in_hbm(needed.reshape(-1)),
        *map(flat, (base, job_res, job_slot, job_cell)),
        *map(in_hbm, (lam_res, lam_work, target_res, target_work)),
    )
    arrived = lax.all_to_all(packed.reshape(devices, rows, 1, LANES), ALL, split_axis=0, concat_axis=0, tiled=True)
    sent, most = pl.pallas_call(
        functools.partial(cell_kernel, dims),
        out_shape=(
            pltpu.VMEM((devices * sent_rows, LANES), F32),
            pltpu.VMEM((1, LANES), F32),
        ),
        in_specs=[vmem],
        out_specs=(vmem, vmem),
        scratch_shapes=[
            pltpu.VMEM((devices, 2 * groups, LANES), jnp.int32),
            pltpu.VMEM((devices, 2 * groups, LANES), F32),
            pltpu.VMEM((devices, groups, LANES), F32),
            pltpu.VMEM((groups, 2 * BLK, reps * LANES), BF16),
            pltpu.VMEM((2 + ITERS + 1, groups * groups, LANES), F32),
        ],
        name="cell",
    )(in_vmem(arrived.reshape(devices * rows, LANES)))
    sent, over = lax.optimization_barrier((sent, (most[0, 0] > dims["cap"]).astype(jnp.int32)))
    back = lax.all_to_all(sent.reshape(devices, sent_rows, 1, LANES), ALL, split_axis=0, concat_axis=0, tiled=True)
    outs = pl.pallas_call(
        functools.partial(join_kernel, dims),
        out_shape=(jax.ShapeDtypeStruct((cells, tracts), F32),) * 4,
        in_specs=[vmem],
        out_specs=(vmem,) * 4,
        name="join",
    )(in_vmem(back.reshape(devices * sent_rows, LANES)))
    return outs, packed, over


def body(mesh_shape, *args):
    base, needed, lam_res = args[0], args[4], args[5]
    shape = needed.shape
    fits, dims = plan_dims(mesh_shape, {"lam": lam_res.shape, "needed": needed.shape, "jobs": base.shape[0]})
    if not fits:
        return start_plan(*args)
    outs, head, over = owner_plan(dims, *args)
    outs, head, over, args = lax.optimization_barrier((outs, head, over, args[:4] + args[5:]))

    def other():
        needed = head[dims["rows"] - 1, : dims["listed"]].astype(jnp.int32).reshape(shape)
        return tuple(start_plan(*args[:4], needed, *args[4:]))

    return lax.cond(over > 0, other, lambda: tuple(outs))


def solution(mesh):
    in_specs = (P(ALL),) * 4 + (P("geo", None, None),) + (P(None, "geo"),) * 4
    out_specs = (P(None, "geo"),) * 4
    return jax.shard_map(
        functools.partial(body, dict(mesh.shape)), mesh=mesh, in_specs=in_specs, out_specs=out_specs, check_vma=False
    )
```

```python
import functools

import jax
import jax.numpy as jnp
from jax import lax
from jax.experimental import pallas as pl
from jax.experimental.pallas import tpu as pltpu
from jax.sharding import PartitionSpec as P

BLK = 32
ITERS = 3
RIDGE = 0.5
LANES = 128
HALVES = 2
ALL = ("geo", "rep")

F32 = jnp.float32
BF16 = jnp.bfloat16


def start_plan(base, job_res, job_slot, job_cell, needed, lam_res, lam_work, target_res, target_work):
    cells, tracts_dev = lam_res.shape
    blocks_dev = tracts_dev // BLK
    requests = lax.all_to_all(needed[0], "geo", split_axis=0, concat_axis=0, tiled=True)
    sources, listed = requests.shape
    onehot = (
        requests[:, :, None] == jnp.arange(blocks_dev, dtype=jnp.int32)[None, None, :]
    ).astype(jnp.float32)
    slot_shape = (sources, listed, cells, BLK)
    slot_count = sources * listed * cells * BLK
    res_index = job_cell * tracts_dev + job_res
    work_index = (job_slot // BLK * cells + job_cell) * BLK + job_slot % BLK

    def serve(table):
        blocks = table.reshape(cells, blocks_dev, BLK).transpose(1, 0, 2)
        return jnp.take(blocks, requests, axis=0)

    def pick(fetched):
        return fetched.reshape(-1)[work_index]

    def fold(arrived):
        return jnp.einsum("skb,skcx->cbx", onehot, arrived, precision=lax.Precision.HIGHEST)

    def totals(values):
        res_part = jax.ops.segment_sum(values, res_index, num_segments=cells * tracts_dev).reshape(
            cells, tracts_dev
        )
        work_part = jax.ops.segment_sum(values, work_index, num_segments=slot_count).reshape(
            slot_shape
        )
        arrived = lax.all_to_all(work_part, "geo", split_axis=0, concat_axis=0, tiled=True)
        folded = fold(arrived)
        return lax.psum((res_part, folded.reshape(cells, tracts_dev)), "rep")

    def inner(a_res, a_work, b_res, b_work):
        return lax.psum(jnp.sum(a_res * b_res) + jnp.sum(a_work * b_work), "geo")

    fetched_lam = lax.all_to_all(serve(lam_work), "geo", split_axis=0, concat_axis=0, tiled=True)
    weight = base * jnp.exp(lam_res.reshape(-1)[res_index] + pick(fetched_lam))
    total_res, total_work = totals(weight)
    resid_res = -(total_res - target_res)
    resid_work = -(total_work - target_work)
    norm = inner(resid_res, resid_work, resid_res, resid_work)
    zeros = jnp.zeros_like(resid_res)

    def turn(_, state):
        step_res, step_work, resid_res, resid_work, dir_res, dir_work, norm_now = state
        dir_piece = lax.all_to_all(serve(dir_work), "geo", split_axis=0, concat_axis=0, tiled=True)
        along = dir_res.reshape(-1)[res_index] + pick(dir_piece)
        image_res, image_work = totals(weight * along)
        image_res = image_res + RIDGE * dir_res
        image_work = image_work + RIDGE * dir_work
        alpha = norm_now / inner(dir_res, dir_work, image_res, image_work)
        step_res = step_res + alpha * dir_res
        step_work = step_work + alpha * dir_work
        resid_res = resid_res - alpha * image_res
        resid_work = resid_work - alpha * image_work
        norm_next = inner(resid_res, resid_work, resid_res, resid_work)
        dir_res = resid_res + norm_next / norm_now * dir_res
        dir_work = resid_work + norm_next / norm_now * dir_work
        return step_res, step_work, resid_res, resid_work, dir_res, dir_work, norm_next

    state = (zeros, zeros, resid_res, resid_work, resid_res, resid_work, norm)
    return lax.fori_loop(0, ITERS, turn, state)[:4]


def split3(x):
    high = x.astype(BF16)
    rest = x - high.astype(F32)
    mid = rest.astype(BF16)
    low = (rest - mid.astype(F32)).astype(BF16)
    return high, mid, low


def dot_nt(a, b):
    return lax.dot_general(a, b, (((1,), (1,)), ((), ())), preferred_element_type=F32)


def dot_nn(a, b):
    return jnp.dot(a, b, preferred_element_type=F32)


def pack_kernel(dims, needed_ref, base_ref, res_ref, slot_ref, cell_ref, a_ref, b_ref, c_ref, d_ref, out_ref):
    devices, rows, cap, listed, cells = dims["devices"], dims["rows"], dims["cap"], dims["listed"], dims["cells"]
    tracts = a_ref.shape[1]
    jobs = cell_ref.shape[1]
    chunk = 256
    cell = cell_ref[...]
    member = lax.broadcasted_iota(jnp.int32, (devices, jobs), 0) == cell
    member_b = member.astype(F32).astype(BF16)
    before = lax.broadcasted_iota(jnp.int32, (chunk, chunk), 0) < lax.broadcasted_iota(jnp.int32, (chunk, chunk), 1)
    before = before.astype(F32).astype(BF16)
    ranks = []
    count = jnp.zeros((devices, 1), F32)
    for at in range(0, jobs, chunk):
        part = member_b[:, at : at + chunk]
        seen = dot_nn(part, before) + count
        own = member[:, at : at + chunk]
        ranks.append(jnp.sum(jnp.where(own, seen, 0.0), axis=0, keepdims=True))
        count = count + jnp.sum(own.astype(F32), axis=1, keepdims=True)
    rank = jnp.concatenate(ranks, axis=1).astype(jnp.int32)
    largest = jnp.max(count, axis=0, keepdims=True)
    chosen = (lax.broadcasted_iota(jnp.int32, (cap, jobs), 0) == rank).astype(F32).astype(BF16)
    values = (res_ref[...].astype(F32), slot_ref[...].astype(F32)) + tuple(x.astype(F32) for x in split3(base_ref[...]))
    held = jnp.concatenate([jnp.where(member, value, 0.0).astype(BF16) for value in values], axis=0)
    moved = dot_nt(held, chosen)
    moved = [moved[k * devices : (k + 1) * devices] for k in range(len(values))]
    sent = (moved[0], moved[1], moved[2] + moved[3] + moved[4])

    def put(row, value):
        out_ref[pl.ds(row, devices, stride=rows), :] = value

    row = 0
    for value in sent:
        put(row, value)
        row += 1
    rep = lax.axis_index("rep")
    mine = a_ref[...]
    for k, ref in enumerate((b_ref, c_ref, d_ref)):
        mine = jnp.where(rep == k + 1, ref[...], mine)
    mine = jnp.concatenate([mine, jnp.zeros((devices - cells, tracts), F32)], axis=0)
    for at in range(0, tracts, LANES):
        put(row, mine[:, at : at + LANES])
        row += 1
    lane = lax.broadcasted_iota(jnp.int32, (devices, LANES), 1)
    head = jnp.broadcast_to(largest, (devices, LANES))
    for p in range(listed):
        head = jnp.where(lane == p, needed_ref[p].astype(F32), head)
    put(row, head)


def cell_kernel(dims, in_ref, out_ref, flag_ref, pick_ref, mask_ref, weight_ref, hot_ref, turn_ref):
    rows, groups, reps, sent_rows = (dims[k] for k in ("rows", "groups", "reps", "sent_rows"))
    at_res, at_slot, at_base, at_own, at_head = 0, 1, 2, 3, 5
    tile = (groups, LANES)
    sub = lax.broadcasted_iota(jnp.int32, tile, 0)
    segment = lax.broadcasted_iota(jnp.int32, tile, 1) // BLK

    side = LANES // BLK

    def row_of(row, device):
        return jnp.broadcast_to(in_ref[pl.ds(device * rows + row, 1), :], tile)

    def shifted(x, segments):
        return pltpu.roll(x, BLK * (segments % side), 1) if segments % side else x

    def unfold(row, rep, place):
        tiles = []
        for half in range(groups // side):
            x = in_ref[pl.ds(rep * rows + row + half, groups, stride=reps * rows), :]
            tiles += [shifted(x, place - k) for k in range(side)]
        return tiles

    def turned(tiles, slot):
        for b, x in enumerate(tiles):
            turn_ref[slot, pl.ds(b, groups, stride=groups), :] = x
        return [turn_ref[slot, pl.ds(g * groups, groups), :] for g in range(groups)]

    def both(res_rep, work_rep, slot):
        res, work = turned(unfold(at_own, res_rep, 0), slot), unfold(at_own, work_rep, 1)
        return [jnp.where(segment == 0, x, jnp.where(segment == 1, y, 0.0)) for x, y in zip(res, work)]

    lane = lax.broadcasted_iota(jnp.int32, tile, 1)
    need = []
    for g in range(groups):
        own = jnp.sum(jnp.where(lane == sub, row_of(at_head, g * reps), 0.0), axis=1, keepdims=True)
        need.append(jnp.where(segment == 1, own, -1.0))

    def fetch(v):
        tables = []
        for g in range(groups):
            table = jnp.where(segment == 0, v[g], 0.0)
            for b in range(groups):
                table = jnp.where(need[g] == float(b), v[b], table)
            tables.append(table)
        return tables

    low = lax.broadcasted_iota(jnp.int32, (BLK, LANES), 0)
    for g in range(groups):
        for r in range(reps):
            device = g * reps + r
            res = row_of(at_res, device).astype(jnp.int32)
            slot = row_of(at_slot, device).astype(jnp.int32)
            pick_ref[device, :groups, :] = res % BLK
            pick_ref[device, groups:, :] = slot % BLK + BLK
            mask_ref[device, :groups, :] = (res // BLK == sub).astype(F32)
            mask_ref[device, groups:, :] = (slot // BLK == sub).astype(F32)
            lanes = slice(r * LANES, (r + 1) * LANES)
            hot_ref[g, :BLK, lanes] = (low == (res % BLK)[:1]).astype(F32).astype(BF16)
            hot_ref[g, BLK:, lanes] = (low == (slot % BLK)[:1]).astype(F32).astype(BF16)

    def along(device, table):
        picked = jnp.take_along_axis(table, pick_ref[device, :groups, :], axis=1) * mask_ref[device, :groups, :]
        picked += jnp.take_along_axis(table, pick_ref[device, groups:, :], axis=1) * mask_ref[device, groups:, :]
        return jnp.broadcast_to(jnp.sum(picked, axis=0, keepdims=True), tile)

    empty = jnp.zeros((2 * groups, LANES - 2 * BLK), F32)

    def scatter(values):
        res, folded = [], [jnp.zeros(tile, F32)] * groups
        for g in range(groups):
            columns = []
            for r in range(reps):
                device = g * reps + r
                mask = mask_ref[device].astype(BF16)
                columns.append(jnp.concatenate([jnp.concatenate([x] * 2, axis=0) * mask for x in split3(values[device])], axis=0))
            sums = dot_nt(jnp.concatenate(columns, axis=1), hot_ref[g])
            sums = sums[: 2 * groups] + sums[2 * groups : 4 * groups] + sums[4 * groups :]
            sums = jnp.concatenate([sums, empty], axis=1)
            res.append(jnp.where(segment == 0, sums[:groups], 0.0))
            for b in range(groups):
                folded[b] = folded[b] + jnp.where(need[g] == float(b), sums[groups:], 0.0)
        return [x + y for x, y in zip(res, folded)]

    lam = fetch(both(0, 1, 0))
    weights = []
    for device in range(groups * reps):
        weight = row_of(at_base, device) * jnp.exp(along(device, lam[device // reps]))
        weight_ref[device] = weight
        weights.append(weight)
    resid = [x - y for x, y in zip(both(2, 3, 1), scatter(weights))]

    def apply(v):
        tables = fetch(v)
        image = scatter([weight_ref[device] * along(device, tables[device // reps]) for device in range(groups * reps)])
        return [x + RIDGE * y for x, y in zip(image, v)]

    def dot(a, b):
        products = [x * y for x, y in zip(a, b)]
        while len(products) > 1:
            products = [x + y for x, y in zip(products[::2], products[1::2])]
        return jnp.sum(jnp.sum(products[0], axis=0, keepdims=True), axis=1, keepdims=True)

    def unit(w):
        square = dot(w, w)
        some = square > 0.0
        scale = jnp.where(some, lax.rsqrt(jnp.where(some, square, 1.0)), 0.0)
        return square * scale, [x * scale for x in w]

    size, v = unit(resid)
    basis, entries = [v], [size]
    last, off = None, None
    for _ in range(ITERS):
        w = apply(v)
        if last is not None:
            w = [x - off * y for x, y in zip(w, last)]
        middle = dot(v, w)
        w = [x - middle * y for x, y in zip(w, v)]
        last = v
        off, v = unit(w)
        entries += [middle, off]
        basis.append(v)

    def put(row, value, which):
        for r in which:
            out_ref[pl.ds(r * sent_rows + row, groups, stride=reps * sent_rows), :] = value

    for k, v in enumerate(basis):
        for part, tiles in enumerate((turned(v, 2 + k), v)):
            for half in range(groups // side):
                row = jnp.zeros(tile, F32)
                for q in range(side):
                    row = jnp.where(segment == q, shifted(tiles[half * side + q], q - part), row)
                put(2 * k + part, row, range(half, reps, HALVES))
    numbers = jnp.zeros(tile, F32)
    for k, entry in enumerate(entries):
        numbers = jnp.where(lane == k, entry, numbers)
    put(sent_rows - 1, numbers, range(reps))
    most = in_ref[pl.ds(at_head, groups * reps, stride=rows), :]
    most = jnp.max(most, axis=0, keepdims=True)
    flag_ref[...] = jnp.broadcast_to(most[:, LANES - 1 :], (1, LANES))


def join_kernel(dims, in_ref, out_ref):
    devices, sent_rows = dims["devices"], dims["sent_rows"]
    tile = (devices, LANES)

    def take(row):
        return in_ref[pl.ds(row, devices, stride=sent_rows), :]

    numbers = take(sent_rows - 1)
    entry = lambda k: jnp.broadcast_to(numbers[:, k : k + 1], tile)
    along = [entry(1 + 2 * k) for k in range(ITERS)]
    off = [entry(2 + 2 * k) for k in range(ITERS)]

    def inner(a, b):
        return jnp.sum(sum(x * y for x, y in zip(a, b)), axis=0, keepdims=True)

    resid = [entry(0)]
    direct = [entry(0)]
    step = []
    norm = inner(resid, resid)
    for turn in range(ITERS):
        image = []
        for k in range(turn + 2):
            value = None
            for term in ((off[k - 1], k - 1), (along[k] if k < ITERS else None, k), (off[k] if k < ITERS else None, k + 1)):
                if 0 <= term[1] <= turn:
                    product = term[0] * direct[term[1]]
                    value = product if value is None else value + product
            image.append(value)
        alpha = norm / inner(direct, image)
        step = [s + alpha * d for s, d in zip(step, direct)] + [alpha * d for d in direct[len(step) :]]
        resid = [r - alpha * i for r, i in zip(resid, image)] + [-alpha * i for i in image[len(resid) :]]
        following = inner(resid, resid)
        beta = following / norm
        direct = [r + beta * d for r, d in zip(resid, direct)] + resid[len(direct) :]
        norm = following

    for part in range(2):
        vectors = [take(2 * k + part) for k in range(ITERS + 1)]
        out_ref[pl.ds(part * devices, devices), :] = sum(s * v for s, v in zip(step, vectors))
        out_ref[pl.ds((2 + part) * devices, devices), :] = sum(r * v for r, v in zip(resid, vectors))


def place_kernel(dims, own_ref, other_ref, *out_refs):
    devices, cells = dims["devices"], dims["cells"]
    first = lax.axis_index("rep") % HALVES == 0
    for k, out_ref in enumerate(out_refs):
        own, other = own_ref[pl.ds(k * devices, devices), :], other_ref[pl.ds(k * devices, devices), :]
        out_ref[:, :LANES] = jnp.where(first, own, other)[:cells]
        out_ref[:, LANES:] = jnp.where(first, other, own)[:cells]


def round_up(value, unit):
    return -(-value // unit) * unit


def plan_dims(mesh_shape, shapes):
    groups, reps = mesh_shape["geo"], mesh_shape["rep"]
    cells, tracts = shapes["lam"]
    listed = shapes["needed"][1] * shapes["needed"][2]
    slots = listed * BLK
    jobs = shapes["jobs"]
    cap = round_up(max(1, 3 * jobs // (2 * cells)), LANES)
    rows = 6
    fits = (
        groups * reps >= cells
        and reps == 4
        and groups == 8
        and listed == groups
        and tracts == groups * BLK == HALVES * LANES
        and cap == LANES
        and jobs % 256 == 0
    )
    return fits, dict(
        devices=groups * reps,
        groups=groups,
        reps=reps,
        cells=cells,
        tracts=tracts,
        listed=listed,
        cap=cap,
        rows=rows,
        sent_rows=2 * (ITERS + 1) + 1,
    )


def owner_plan(dims, base, job_res, job_slot, job_cell, needed, lam_res, lam_work, target_res, target_work):
    devices, rows, sent_rows, cells, tracts, groups, reps = (
        dims[k] for k in ("devices", "rows", "sent_rows", "cells", "tracts", "groups", "reps")
    )
    vmem = pl.BlockSpec(memory_space=pltpu.VMEM)
    smem = pl.BlockSpec(memory_space=pltpu.SMEM)
    flat = lambda x: in_hbm(x.reshape(1, -1))
    in_hbm = lambda x: pltpu.with_memory_space_constraint(x, pltpu.HBM)
    in_vmem = lambda x: pltpu.with_memory_space_constraint(x, pltpu.VMEM)
    packed = pl.pallas_call(
        functools.partial(pack_kernel, dims),
        out_shape=pltpu.VMEM((devices * rows, LANES), F32),
        in_specs=[smem] + [vmem] * 8,
        out_specs=vmem,
        name="pack",
    )(
        in_hbm(needed.reshape(-1)),
        *map(flat, (base, job_res, job_slot, job_cell)),
        *map(in_hbm, (lam_res, lam_work, target_res, target_work)),
    )
    arrived = lax.all_to_all(packed.reshape(devices, rows, 1, LANES), ALL, split_axis=0, concat_axis=0, tiled=True)
    sent, most = pl.pallas_call(
        functools.partial(cell_kernel, dims),
        out_shape=(
            pltpu.VMEM((devices * sent_rows, LANES), F32),
            pltpu.VMEM((1, LANES), F32),
        ),
        in_specs=[vmem],
        out_specs=(vmem, vmem),
        scratch_shapes=[
            pltpu.VMEM((devices, 2 * groups, LANES), jnp.int32),
            pltpu.VMEM((devices, 2 * groups, LANES), F32),
            pltpu.VMEM((devices, groups, LANES), F32),
            pltpu.VMEM((groups, 2 * BLK, reps * LANES), BF16),
            pltpu.VMEM((2 + ITERS + 1, groups * groups, LANES), F32),
        ],
        name="cell",
    )(in_vmem(arrived.reshape(devices * rows, LANES)))
    sent, over = lax.optimization_barrier((sent, (most[0, 0] > dims["cap"]).astype(jnp.int32)))
    back = lax.all_to_all(sent.reshape(devices, sent_rows, 1, LANES), ALL, split_axis=0, concat_axis=0, tiled=True)
    own = pl.pallas_call(
        functools.partial(join_kernel, dims),
        out_shape=pltpu.VMEM((4 * devices, LANES), F32),
        in_specs=[vmem],
        out_specs=vmem,
        name="join",
    )(in_vmem(back.reshape(devices * sent_rows, LANES)))
    other = lax.ppermute(own, "rep", [(r, r ^ 1) for r in range(reps)])
    outs = pl.pallas_call(
        functools.partial(place_kernel, dims),
        out_shape=(jax.ShapeDtypeStruct((cells, tracts), F32),) * 4,
        in_specs=[vmem] * 2,
        out_specs=(vmem,) * 4,
        name="place",
    )(in_vmem(own), in_vmem(other))
    return outs, packed, over


def body(mesh_shape, *args):
    base, needed, lam_res = args[0], args[4], args[5]
    shape = needed.shape
    fits, dims = plan_dims(mesh_shape, {"lam": lam_res.shape, "needed": needed.shape, "jobs": base.shape[0]})
    if not fits:
        return start_plan(*args)
    outs, head, over = owner_plan(dims, *args)
    outs, head, over, args = lax.optimization_barrier((outs, head, over, args[:4] + args[5:]))

    def other():
        needed = head[dims["rows"] - 1, : dims["listed"]].astype(jnp.int32).reshape(shape)
        return tuple(start_plan(*args[:4], needed, *args[4:]))

    return lax.cond(over > 0, other, lambda: tuple(outs))


def solution(mesh):
    in_specs = (P(ALL),) * 4 + (P("geo", None, None),) + (P(None, "geo"),) * 4
    out_specs = (P(None, "geo"),) * 4
    return jax.shard_map(
        functools.partial(body, dict(mesh.shape)), mesh=mesh, in_specs=in_specs, out_specs=out_specs, check_vma=False
    )
```

```python
import functools

import jax
import jax.numpy as jnp
from jax import lax
from jax.experimental import pallas as pl
from jax.experimental.pallas import tpu as pltpu
from jax.sharding import PartitionSpec as P

BLK = 32
ITERS = 3
RIDGE = 0.5
LANES = 128
HALVES = 2
ALL = ("geo", "rep")

F32 = jnp.float32
BF16 = jnp.bfloat16


def start_plan(base, job_res, job_slot, job_cell, needed, lam_res, lam_work, target_res, target_work):
    cells, tracts_dev = lam_res.shape
    blocks_dev = tracts_dev // BLK
    requests = lax.all_to_all(needed[0], "geo", split_axis=0, concat_axis=0, tiled=True)
    sources, listed = requests.shape
    onehot = (
        requests[:, :, None] == jnp.arange(blocks_dev, dtype=jnp.int32)[None, None, :]
    ).astype(jnp.float32)
    slot_shape = (sources, listed, cells, BLK)
    slot_count = sources * listed * cells * BLK
    res_index = job_cell * tracts_dev + job_res
    work_index = (job_slot // BLK * cells + job_cell) * BLK + job_slot % BLK

    def serve(table):
        blocks = table.reshape(cells, blocks_dev, BLK).transpose(1, 0, 2)
        return jnp.take(blocks, requests, axis=0)

    def pick(fetched):
        return fetched.reshape(-1)[work_index]

    def fold(arrived):
        return jnp.einsum("skb,skcx->cbx", onehot, arrived, precision=lax.Precision.HIGHEST)

    def totals(values):
        res_part = jax.ops.segment_sum(values, res_index, num_segments=cells * tracts_dev).reshape(
            cells, tracts_dev
        )
        work_part = jax.ops.segment_sum(values, work_index, num_segments=slot_count).reshape(
            slot_shape
        )
        arrived = lax.all_to_all(work_part, "geo", split_axis=0, concat_axis=0, tiled=True)
        folded = fold(arrived)
        return lax.psum((res_part, folded.reshape(cells, tracts_dev)), "rep")

    def inner(a_res, a_work, b_res, b_work):
        return lax.psum(jnp.sum(a_res * b_res) + jnp.sum(a_work * b_work), "geo")

    fetched_lam = lax.all_to_all(serve(lam_work), "geo", split_axis=0, concat_axis=0, tiled=True)
    weight = base * jnp.exp(lam_res.reshape(-1)[res_index] + pick(fetched_lam))
    total_res, total_work = totals(weight)
    resid_res = -(total_res - target_res)
    resid_work = -(total_work - target_work)
    norm = inner(resid_res, resid_work, resid_res, resid_work)
    zeros = jnp.zeros_like(resid_res)

    def turn(_, state):
        step_res, step_work, resid_res, resid_work, dir_res, dir_work, norm_now = state
        dir_piece = lax.all_to_all(serve(dir_work), "geo", split_axis=0, concat_axis=0, tiled=True)
        along = dir_res.reshape(-1)[res_index] + pick(dir_piece)
        image_res, image_work = totals(weight * along)
        image_res = image_res + RIDGE * dir_res
        image_work = image_work + RIDGE * dir_work
        alpha = norm_now / inner(dir_res, dir_work, image_res, image_work)
        step_res = step_res + alpha * dir_res
        step_work = step_work + alpha * dir_work
        resid_res = resid_res - alpha * image_res
        resid_work = resid_work - alpha * image_work
        norm_next = inner(resid_res, resid_work, resid_res, resid_work)
        dir_res = resid_res + norm_next / norm_now * dir_res
        dir_work = resid_work + norm_next / norm_now * dir_work
        return step_res, step_work, resid_res, resid_work, dir_res, dir_work, norm_next

    state = (zeros, zeros, resid_res, resid_work, resid_res, resid_work, norm)
    return lax.fori_loop(0, ITERS, turn, state)[:4]


def split3(x):
    high = x.astype(BF16)
    rest = x - high.astype(F32)
    mid = rest.astype(BF16)
    low = (rest - mid.astype(F32)).astype(BF16)
    return high, mid, low


def dot_nt(a, b):
    return lax.dot_general(a, b, (((1,), (1,)), ((), ())), preferred_element_type=F32)


def dot_nn(a, b):
    return jnp.dot(a, b, preferred_element_type=F32)


def pack_kernel(dims, needed_ref, base_ref, res_ref, slot_ref, cell_ref, a_ref, b_ref, c_ref, d_ref, out_ref):
    devices, rows, cap, listed, cells = dims["devices"], dims["rows"], dims["cap"], dims["listed"], dims["cells"]
    tracts = a_ref.shape[1]
    jobs = cell_ref.shape[1]
    chunk = 256
    cell = cell_ref[...]
    member = lax.broadcasted_iota(jnp.int32, (devices, jobs), 0) == cell
    member_b = member.astype(F32).astype(BF16)
    before = lax.broadcasted_iota(jnp.int32, (chunk, chunk), 0) < lax.broadcasted_iota(jnp.int32, (chunk, chunk), 1)
    before = before.astype(F32).astype(BF16)
    ranks = []
    count = jnp.zeros((devices, 1), F32)
    for at in range(0, jobs, chunk):
        part = member_b[:, at : at + chunk]
        seen = dot_nn(part, before) + count
        own = member[:, at : at + chunk]
        ranks.append(jnp.sum(jnp.where(own, seen, 0.0), axis=0, keepdims=True))
        count = count + jnp.sum(own.astype(F32), axis=1, keepdims=True)
    rank = jnp.concatenate(ranks, axis=1).astype(jnp.int32)
    largest = jnp.max(count, axis=0, keepdims=True)
    chosen = (lax.broadcasted_iota(jnp.int32, (cap, jobs), 0) == rank).astype(F32).astype(BF16)
    values = (res_ref[...].astype(F32), slot_ref[...].astype(F32)) + tuple(x.astype(F32) for x in split3(base_ref[...]))
    held = jnp.concatenate([jnp.where(member, value, 0.0).astype(BF16) for value in values], axis=0)
    moved = dot_nt(held, chosen)
    moved = [moved[k * devices : (k + 1) * devices] for k in range(len(values))]
    sent = (moved[0], moved[1], moved[2] + moved[3] + moved[4])

    def put(row, value):
        out_ref[pl.ds(row, devices, stride=rows), :] = value

    row = 0
    for value in sent:
        put(row, value)
        row += 1
    rep = lax.axis_index("rep")
    mine = a_ref[...]
    for k, ref in enumerate((b_ref, c_ref, d_ref)):
        mine = jnp.where(rep == k + 1, ref[...], mine)
    mine = jnp.concatenate([mine, jnp.zeros((devices - cells, tracts), F32)], axis=0)
    for at in range(0, tracts, LANES):
        put(row, mine[:, at : at + LANES])
        row += 1
    lane = lax.broadcasted_iota(jnp.int32, (devices, LANES), 1)
    head = jnp.broadcast_to(largest, (devices, LANES))
    for p in range(listed):
        head = jnp.where(lane == p, needed_ref[p].astype(F32), head)
    put(row, head)


def cell_kernel(dims, in_ref, out_ref, flag_ref, digit_ref, mask_ref, hot_ref, part_ref, turn_ref):
    rows, groups, reps, sent_rows = (dims[k] for k in ("rows", "groups", "reps", "sent_rows"))
    at_res, at_slot, at_base, at_own, at_head = 0, 1, 2, 3, 5
    tile = (groups, LANES)
    side = LANES // BLK
    sub = lax.broadcasted_iota(jnp.int32, tile, 0)
    lane = lax.broadcasted_iota(jnp.int32, tile, 1)
    segment = lane // BLK

    def of_groups(row, rep):
        return in_ref[pl.ds(rep * rows + row, groups, stride=reps * rows), :]

    def shifted(x, segments):
        return pltpu.roll(x, BLK * (segments % side), 1) if segments % side else x

    def unfold(rep, place):
        tiles = []
        for half in range(groups // side):
            x = of_groups(at_own + half, rep)
            tiles += [shifted(x, place - k) for k in range(side)]
        return tiles

    def turned(tiles, slot):
        for b, x in enumerate(tiles):
            turn_ref[slot, pl.ds(b, groups, stride=groups), :] = x
        return [turn_ref[slot, pl.ds(g * groups, groups), :] for g in range(groups)]

    head = of_groups(at_head, 0)
    halves = range(groups // side)
    choose = [jnp.take_along_axis(head, half * side + segment, axis=1).astype(jnp.int32) for half in halves]
    need = []
    for g in range(groups):
        row = jnp.broadcast_to(in_ref[pl.ds(g * reps * rows + at_head, 1), :], tile)
        listed = jnp.sum(jnp.where(lane == sub, row, 0.0), axis=1, keepdims=True)
        need.append(jnp.where(segment == 1, listed, -1.0))

    tracts = [[of_groups(row, r).astype(jnp.int32) for r in range(reps)] for row in (at_res, at_slot)]
    for kind in range(2):
        for r, x in enumerate(tracts[kind]):
            digit_ref[2 * kind, pl.ds(r * groups, groups), :] = (x & (BLK - 1)).astype(F32)
            high = lax.shift_right_logical(x, BLK.bit_length() - 1)
            digit_ref[2 * kind + 1, pl.ds(r * groups, groups), :] = high.astype(F32)

    place = lax.broadcasted_iota(jnp.int32, (BLK, LANES), 0).astype(F32).astype(BF16)
    sub_f = sub.astype(F32)
    one, none = jnp.ones((BLK, LANES), BF16), jnp.zeros((BLK, LANES), BF16)
    for g in range(groups):
        for r in range(reps):
            lanes = slice(r * LANES, (r + 1) * LANES)
            masks = []
            for kind in range(2):
                digit = lambda k: digit_ref[2 * kind + k, pl.ds(r * groups + g, 1), :]
                masks.append((jnp.broadcast_to(digit(1), tile) == sub_f).astype(F32))
                spot = jnp.broadcast_to(digit(0), (BLK, LANES)).astype(BF16)
                hot_ref[g, kind * BLK : (kind + 1) * BLK, lanes] = jnp.where(spot == place, one, none)
            mask_ref[g, :, lanes] = jnp.concatenate(masks, axis=0).astype(BF16)

    def folded(tiles, place):
        out = []
        for half in halves:
            x = shifted(tiles[half * side], -place)
            for q in range(1, side):
                x = jnp.where(segment == q, shifted(tiles[half * side + q], q - place), x)
            out.append(x)
        return out

    def along(res, owned):
        work = [jnp.take_along_axis(x, chosen, axis=0) for x, chosen in zip(owned, choose)]
        out = []
        for r in range(reps):
            value = 0.0
            for table, tract in ((res, tracts[0][r]), (work, tracts[1][r])):
                spot = tract & (LANES - 1)
                first, second = (jnp.take_along_axis(x, spot, axis=1) for x in table)
                value += jnp.where(tract < LANES, first, second)
            out.append(value)
        return out

    empty = jnp.zeros((2 * groups, LANES - 2 * BLK), F32)

    def scatter(values, slot):
        for r in range(reps):
            for k, x in enumerate(split3(values[r])):
                part_ref[slot, k, pl.ds(r * groups, groups), :] = x.astype(F32)
        res, work = [], [jnp.zeros(tile, F32)] * groups
        for g in range(groups):
            columns = []
            for r in range(reps):
                mask = mask_ref[g, :, r * LANES : (r + 1) * LANES]
                parts = [
                    jnp.broadcast_to(part_ref[slot, k, pl.ds(r * groups + g, 1), :], (2 * groups, LANES)).astype(BF16)
                    for k in range(3)
                ]
                columns.append(jnp.concatenate([x * mask for x in parts], axis=0))
            sums = dot_nt(jnp.concatenate(columns, axis=1), hot_ref[g])
            sums = sums[: 2 * groups] + sums[2 * groups : 4 * groups] + sums[4 * groups :]
            sums = jnp.concatenate([sums, empty], axis=1)
            res.append(jnp.where(segment == 0, sums[:groups], 0.0))
            for b in range(groups):
                work[b] = work[b] + jnp.where(need[g] == float(b), sums[groups:], 0.0)
        return [x + y for x, y in zip(res, work)]

    def dot(a, b):
        products = [x * y for x, y in zip(a, b)]
        while len(products) > 1:
            products = [x + y for x, y in zip(products[::2], products[1::2])]
        return jnp.sum(jnp.sum(products[0], axis=0, keepdims=True), axis=1, keepdims=True)

    def ratio(a, b):
        return jnp.where(b > 0.0, a / jnp.where(b > 0.0, b, 1.0), 0.0)

    def put(row, value, which):
        for r in which:
            out_ref[pl.ds(r * sent_rows + row, groups, stride=reps * sent_rows), :] = value

    def own_rows(rep):
        return [of_groups(at_own + half, rep) for half in halves]

    def owned(rep, slot):
        return folded(turned(unfold(rep, 0), slot), 0)

    weight = [of_groups(at_base, r) * jnp.exp(x) for r, x in enumerate(along(own_rows(0), owned(1, 0)))]
    v = own_rows(2) + own_rows(3)
    on_jobs = along(own_rows(2), owned(3, 1))
    last = last_on_jobs = None
    sizes, middles, scales, backs = [], [], [], []
    for k in range(ITERS + 1):
        if k:
            q = [x * y for x, y in zip(weight, on_jobs)]
            sizes.append(dot(v, v))
            middles.append(ratio(dot(q, on_jobs), sizes[-1]))
        tiles = scatter(q if k else weight, k)
        rows_of_w = turned(tiles, 2 + k)
        res = folded(rows_of_w, 0)
        w = res + folded(tiles, 1)
        w_on_jobs = along(res, folded(rows_of_w, 1))
        if k:
            square = dot(tiles, tiles)
            scale = jnp.where(square > 0.0, lax.rsqrt(jnp.where(square > 0.0, square, 1.0)), 0.0)
            if last is not None:
                backs.append(ratio(scales[-1] * sizes[-1], sizes[-2]))
            scales.append(square * scale)

            def step(x, y, z):
                out = x - middles[-1] * y
                return scale * (out if z is None else out - backs[-1] * z)

            nothing = [None] * max(len(v), reps)
            following = [step(*t) for t in zip(w, v, last or nothing)]
            following_on_jobs = [step(*t) for t in zip(w_on_jobs, on_jobs, last_on_jobs or nothing)]
            last, last_on_jobs = v, on_jobs
        else:
            following = [y - x for x, y in zip(w, v)]
            following_on_jobs = [y - x for x, y in zip(w_on_jobs, on_jobs)]
        v, on_jobs = following, following_on_jobs
        for part in range(2):
            for half in halves:
                put(2 * k + part, v[part * len(halves) + half], range(half, reps, HALVES))
    numbers = jnp.zeros(tile, F32)
    for k, entry in enumerate(sizes + middles + scales + backs):
        numbers = jnp.where(lane == k, entry, numbers)
    put(sent_rows - 1, numbers, range(reps))
    most = in_ref[pl.ds(at_head, groups * reps, stride=rows), :]
    most = jnp.max(most, axis=0, keepdims=True)
    flag_ref[...] = jnp.broadcast_to(most[:, LANES - 1 :], (1, LANES))


def join_kernel(dims, in_ref, out_ref):
    devices, sent_rows = dims["devices"], dims["sent_rows"]
    tile = (devices, LANES)

    def take(row):
        return in_ref[pl.ds(row, devices, stride=sent_rows), :]

    numbers = take(sent_rows - 1)
    entry = lambda k: jnp.broadcast_to(numbers[:, k : k + 1], tile)
    sizes, middles, scales, backs = ([entry(k * ITERS + j) for j in range(ITERS - (k == 3))] for k in range(4))

    def inner(a, b):
        return jnp.sum(sum(g * (x * y) for g, x, y in zip(sizes, a, b)), axis=0, keepdims=True)

    resid = [jnp.ones(tile, F32)]
    direct = list(resid)
    step = []
    norm = inner(resid, resid)
    for turn in range(ITERS):
        image = []
        for k in range(turn + 2):
            terms = []
            if k:
                terms.append(scales[k - 1] * direct[k - 1])
            if k <= turn:
                terms.append((middles[k] + RIDGE) * direct[k])
            if k < turn:
                terms.append(backs[k] * direct[k + 1])
            image.append(sum(terms))
        alpha = norm / inner(direct, image)
        step = [s + alpha * d for s, d in zip(step, direct)] + [alpha * d for d in direct[len(step) :]]
        resid = [r - alpha * i for r, i in zip(resid, image)] + [-alpha * i for i in image[len(resid) :]]
        if turn + 1 < ITERS:
            following = inner(resid, resid)
            beta = following / norm
            direct = [r + beta * d for r, d in zip(resid, direct)] + resid[len(direct) :]
            norm = following

    for part in range(2):
        vectors = [take(2 * k + part) for k in range(ITERS + 1)]
        out_ref[pl.ds(part * devices, devices), :] = sum(s * v for s, v in zip(step, vectors))
        out_ref[pl.ds((2 + part) * devices, devices), :] = sum(r * v for r, v in zip(resid, vectors))


def place_kernel(dims, own_ref, other_ref, *out_refs):
    devices, cells = dims["devices"], dims["cells"]
    first = lax.axis_index("rep") % HALVES == 0
    for k, out_ref in enumerate(out_refs):
        own, other = own_ref[pl.ds(k * devices, devices), :], other_ref[pl.ds(k * devices, devices), :]
        out_ref[:, :LANES] = jnp.where(first, own, other)[:cells]
        out_ref[:, LANES:] = jnp.where(first, other, own)[:cells]


def round_up(value, unit):
    return -(-value // unit) * unit


def plan_dims(mesh_shape, shapes):
    groups, reps = mesh_shape["geo"], mesh_shape["rep"]
    cells, tracts = shapes["lam"]
    listed = shapes["needed"][1] * shapes["needed"][2]
    slots = listed * BLK
    jobs = shapes["jobs"]
    cap = round_up(max(1, 3 * jobs // (2 * cells)), LANES)
    rows = 6
    fits = (
        groups * reps >= cells
        and reps == 4
        and groups == 8
        and listed == groups
        and tracts == groups * BLK == HALVES * LANES
        and cap == LANES
        and jobs % 256 == 0
    )
    return fits, dict(
        devices=groups * reps,
        groups=groups,
        reps=reps,
        cells=cells,
        tracts=tracts,
        listed=listed,
        cap=cap,
        rows=rows,
        sent_rows=2 * (ITERS + 1) + 1,
    )


def owner_plan(dims, base, job_res, job_slot, job_cell, needed, lam_res, lam_work, target_res, target_work):
    devices, rows, sent_rows, cells, tracts, groups, reps = (
        dims[k] for k in ("devices", "rows", "sent_rows", "cells", "tracts", "groups", "reps")
    )
    vmem = pl.BlockSpec(memory_space=pltpu.VMEM)
    smem = pl.BlockSpec(memory_space=pltpu.SMEM)
    flat = lambda x: in_hbm(x.reshape(1, -1))
    in_hbm = lambda x: pltpu.with_memory_space_constraint(x, pltpu.HBM)
    in_vmem = lambda x: pltpu.with_memory_space_constraint(x, pltpu.VMEM)
    packed = pl.pallas_call(
        functools.partial(pack_kernel, dims),
        out_shape=pltpu.VMEM((devices * rows, LANES), F32),
        in_specs=[smem] + [vmem] * 8,
        out_specs=vmem,
        name="pack",
    )(
        in_hbm(needed.reshape(-1)),
        *map(flat, (base, job_res, job_slot, job_cell)),
        *map(in_hbm, (lam_res, lam_work, target_res, target_work)),
    )
    arrived = lax.all_to_all(packed.reshape(devices, rows, 1, LANES), ALL, split_axis=0, concat_axis=0, tiled=True)
    sent, most = pl.pallas_call(
        functools.partial(cell_kernel, dims),
        out_shape=(
            pltpu.VMEM((devices * sent_rows, LANES), F32),
            pltpu.VMEM((1, LANES), F32),
        ),
        in_specs=[vmem],
        out_specs=(vmem, vmem),
        scratch_shapes=[
            pltpu.VMEM((4, devices, LANES), F32),
            pltpu.VMEM((groups, 2 * groups, reps * LANES), BF16),
            pltpu.VMEM((groups, 2 * BLK, reps * LANES), BF16),
            pltpu.VMEM((ITERS + 1, 3, devices, LANES), F32),
            pltpu.VMEM((2 + ITERS + 1, groups * groups, LANES), F32),
        ],
        name="cell",
    )(in_vmem(arrived.reshape(devices * rows, LANES)))
    sent, over = lax.optimization_barrier((sent, (most[0, 0] > dims["cap"]).astype(jnp.int32)))
    back = lax.all_to_all(sent.reshape(devices, sent_rows, 1, LANES), ALL, split_axis=0, concat_axis=0, tiled=True)
    own = pl.pallas_call(
        functools.partial(join_kernel, dims),
        out_shape=pltpu.VMEM((4 * devices, LANES), F32),
        in_specs=[vmem],
        out_specs=vmem,
        name="join",
    )(in_vmem(back.reshape(devices * sent_rows, LANES)))
    other = lax.ppermute(own, "rep", [(r, r ^ 1) for r in range(reps)])
    outs = pl.pallas_call(
        functools.partial(place_kernel, dims),
        out_shape=(jax.ShapeDtypeStruct((cells, tracts), F32),) * 4,
        in_specs=[vmem] * 2,
        out_specs=(vmem,) * 4,
        name="place",
    )(in_vmem(own), in_vmem(other))
    return outs, packed, over


def body(mesh_shape, *args):
    base, needed, lam_res = args[0], args[4], args[5]
    shape = needed.shape
    fits, dims = plan_dims(mesh_shape, {"lam": lam_res.shape, "needed": needed.shape, "jobs": base.shape[0]})
    if not fits:
        return start_plan(*args)
    outs, head, over = owner_plan(dims, *args)
    outs, head, over, args = lax.optimization_barrier((outs, head, over, args[:4] + args[5:]))

    def other():
        needed = head[dims["rows"] - 1, : dims["listed"]].astype(jnp.int32).reshape(shape)
        return tuple(start_plan(*args[:4], needed, *args[4:]))

    return lax.cond(over > 0, other, lambda: tuple(outs))


def solution(mesh):
    in_specs = (P(ALL),) * 4 + (P("geo", None, None),) + (P(None, "geo"),) * 4
    out_specs = (P(None, "geo"),) * 4
    return jax.shard_map(
        functools.partial(body, dict(mesh.shape)), mesh=mesh, in_specs=in_specs, out_specs=out_specs, check_vma=False
    )
```

```python
import functools

import jax
import jax.numpy as jnp
from jax import lax
from jax.experimental import pallas as pl
from jax.experimental.pallas import tpu as pltpu
from jax.sharding import PartitionSpec as P

BLK = 32
ITERS = 3
RIDGE = 0.5
LANES = 128
HALVES = 2
ALL = ("geo", "rep")

F32 = jnp.float32
BF16 = jnp.bfloat16


def start_plan(base, job_res, job_slot, job_cell, needed, lam_res, lam_work, target_res, target_work):
    cells, tracts_dev = lam_res.shape
    blocks_dev = tracts_dev // BLK
    requests = lax.all_to_all(needed[0], "geo", split_axis=0, concat_axis=0, tiled=True)
    sources, listed = requests.shape
    onehot = (
        requests[:, :, None] == jnp.arange(blocks_dev, dtype=jnp.int32)[None, None, :]
    ).astype(jnp.float32)
    slot_shape = (sources, listed, cells, BLK)
    slot_count = sources * listed * cells * BLK
    res_index = job_cell * tracts_dev + job_res
    work_index = (job_slot // BLK * cells + job_cell) * BLK + job_slot % BLK

    def serve(table):
        blocks = table.reshape(cells, blocks_dev, BLK).transpose(1, 0, 2)
        return jnp.take(blocks, requests, axis=0)

    def pick(fetched):
        return fetched.reshape(-1)[work_index]

    def fold(arrived):
        return jnp.einsum("skb,skcx->cbx", onehot, arrived, precision=lax.Precision.HIGHEST)

    def totals(values):
        res_part = jax.ops.segment_sum(values, res_index, num_segments=cells * tracts_dev).reshape(
            cells, tracts_dev
        )
        work_part = jax.ops.segment_sum(values, work_index, num_segments=slot_count).reshape(
            slot_shape
        )
        arrived = lax.all_to_all(work_part, "geo", split_axis=0, concat_axis=0, tiled=True)
        folded = fold(arrived)
        return lax.psum((res_part, folded.reshape(cells, tracts_dev)), "rep")

    def inner(a_res, a_work, b_res, b_work):
        return lax.psum(jnp.sum(a_res * b_res) + jnp.sum(a_work * b_work), "geo")

    fetched_lam = lax.all_to_all(serve(lam_work), "geo", split_axis=0, concat_axis=0, tiled=True)
    weight = base * jnp.exp(lam_res.reshape(-1)[res_index] + pick(fetched_lam))
    total_res, total_work = totals(weight)
    resid_res = -(total_res - target_res)
    resid_work = -(total_work - target_work)
    norm = inner(resid_res, resid_work, resid_res, resid_work)
    zeros = jnp.zeros_like(resid_res)

    def turn(_, state):
        step_res, step_work, resid_res, resid_work, dir_res, dir_work, norm_now = state
        dir_piece = lax.all_to_all(serve(dir_work), "geo", split_axis=0, concat_axis=0, tiled=True)
        along = dir_res.reshape(-1)[res_index] + pick(dir_piece)
        image_res, image_work = totals(weight * along)
        image_res = image_res + RIDGE * dir_res
        image_work = image_work + RIDGE * dir_work
        alpha = norm_now / inner(dir_res, dir_work, image_res, image_work)
        step_res = step_res + alpha * dir_res
        step_work = step_work + alpha * dir_work
        resid_res = resid_res - alpha * image_res
        resid_work = resid_work - alpha * image_work
        norm_next = inner(resid_res, resid_work, resid_res, resid_work)
        dir_res = resid_res + norm_next / norm_now * dir_res
        dir_work = resid_work + norm_next / norm_now * dir_work
        return step_res, step_work, resid_res, resid_work, dir_res, dir_work, norm_next

    state = (zeros, zeros, resid_res, resid_work, resid_res, resid_work, norm)
    return lax.fori_loop(0, ITERS, turn, state)[:4]


def split3(x):
    high = x.astype(BF16)
    rest = x - high.astype(F32)
    mid = rest.astype(BF16)
    low = (rest - mid.astype(F32)).astype(BF16)
    return high, mid, low


def dot_nt(a, b):
    return lax.dot_general(a, b, (((1,), (1,)), ((), ())), preferred_element_type=F32)


def dot_nn(a, b):
    return jnp.dot(a, b, preferred_element_type=F32)


def pack_kernel(dims, needed_ref, base_ref, res_ref, slot_ref, cell_ref, a_ref, b_ref, c_ref, d_ref, out_ref):
    devices, rows, cap, listed, cells = dims["devices"], dims["rows"], dims["cap"], dims["listed"], dims["cells"]
    tracts = a_ref.shape[1]
    jobs = cell_ref.shape[1]
    chunk = 256
    cell = cell_ref[...]
    member = lax.broadcasted_iota(jnp.int32, (devices, jobs), 0) == cell
    narrow = lambda x, n: jnp.broadcast_to(x.astype(F32), (n, jobs)).astype(BF16)
    number = lambda n: lax.broadcasted_iota(jnp.int32, (n, jobs), 0).astype(F32).astype(BF16)
    one, none = (lambda n: jnp.ones((n, jobs), BF16)), (lambda n: jnp.zeros((n, jobs), BF16))
    member_n = number(devices) == narrow(cell, devices)
    member_b = jnp.where(member_n, one(devices), none(devices))
    before = lax.broadcasted_iota(jnp.int32, (chunk, chunk), 0) < lax.broadcasted_iota(jnp.int32, (chunk, chunk), 1)
    before = before.astype(F32).astype(BF16)
    ranks = []
    count = jnp.zeros((devices, 1), F32)
    for at in range(0, jobs, chunk):
        part = member_b[:, at : at + chunk]
        seen = dot_nn(part, before) + count
        own = member[:, at : at + chunk]
        ranks.append(jnp.sum(jnp.where(own, seen, 0.0), axis=0, keepdims=True))
        count = count + jnp.sum(own.astype(F32), axis=1, keepdims=True)
    rank = jnp.concatenate(ranks, axis=1).astype(jnp.int32)
    largest = jnp.max(count, axis=0, keepdims=True)
    rank = jnp.where(rank < cap, rank, LANES)
    chosen = jnp.where(number(LANES) == narrow(rank, LANES), one(LANES), none(LANES))
    values = (res_ref[...].astype(F32), slot_ref[...].astype(F32)) + tuple(x.astype(F32) for x in split3(base_ref[...]))
    held = jnp.concatenate([jnp.where(member_n, narrow(value, devices), none(devices)) for value in values], axis=0)
    moved = dot_nt(held, chosen)
    moved = [moved[k * devices : (k + 1) * devices] for k in range(len(values))]
    lane = lax.broadcasted_iota(jnp.int32, (devices, LANES), 1)
    head = jnp.zeros((devices, LANES), F32)
    for p in range(listed):
        head = jnp.where(lane == cap + p, needed_ref[p].astype(F32), head)
    sent = (moved[0] + head, jnp.where(lane < cap, moved[1], largest), moved[2] + moved[3] + moved[4])

    def put(row, value):
        out_ref[pl.ds(row, devices, stride=rows), :] = value

    row = 0
    for value in sent:
        put(row, value)
        row += 1
    rep = lax.axis_index("rep")
    mine = a_ref[...]
    for k, ref in enumerate((b_ref, c_ref, d_ref)):
        mine = jnp.where(rep == k + 1, ref[...], mine)
    mine = jnp.concatenate([mine, jnp.zeros((devices - cells, tracts), F32)], axis=0)
    for at in range(0, tracts, LANES):
        put(row, mine[:, at : at + LANES])
        row += 1


def cell_kernel(dims, in_ref, out_ref, flag_ref, digit_ref, mask_ref, hot_ref, part_ref, turn_ref):
    rows, groups, reps, sent_rows, cap = (dims[k] for k in ("rows", "groups", "reps", "sent_rows", "cap"))
    at_res, at_slot, at_base, at_own = 0, 1, 2, 3
    tile = (groups, LANES)
    side = LANES // BLK
    sub = lax.broadcasted_iota(jnp.int32, tile, 0)
    lane = lax.broadcasted_iota(jnp.int32, tile, 1)
    segment = lane // BLK

    def of_groups(row, rep):
        return in_ref[pl.ds(rep * rows + row, groups, stride=reps * rows), :]

    def shifted(x, segments):
        return pltpu.roll(x, BLK * (segments % side), 1) if segments % side else x

    def unfold(rep, place):
        tiles = []
        for half in range(groups // side):
            x = of_groups(at_own + half, rep)
            tiles += [shifted(x, place - k) for k in range(side)]
        return tiles

    def turned(tiles, slot):
        for b, x in enumerate(tiles):
            turn_ref[slot, pl.ds(b, groups, stride=groups), :] = x
        return [turn_ref[slot, pl.ds(g * groups, groups), :] for g in range(groups)]

    head = of_groups(at_res, 0)
    halves = range(groups // side)
    choose = [jnp.take_along_axis(head, cap + half * side + segment, axis=1).astype(jnp.int32) for half in halves]
    need = []
    for g in range(groups):
        row = jnp.broadcast_to(in_ref[pl.ds(g * reps * rows + at_res, 1), :], tile)
        listed = jnp.sum(jnp.where(lane == cap + sub, row, 0.0), axis=1, keepdims=True)
        need.append(jnp.where(segment == 1, listed, -1.0))

    tracts = [[of_groups(row, r).astype(jnp.int32) for r in range(reps)] for row in (at_res, at_slot)]
    for kind in range(2):
        for r, x in enumerate(tracts[kind]):
            digit_ref[2 * kind, pl.ds(r * groups, groups), :] = (x & (BLK - 1)).astype(F32)
            high = lax.shift_right_logical(x, BLK.bit_length() - 1)
            digit_ref[2 * kind + 1, pl.ds(r * groups, groups), :] = high.astype(F32)

    place = lax.broadcasted_iota(jnp.int32, (BLK, LANES), 0).astype(F32).astype(BF16)
    sub_f = sub.astype(F32)
    one, none = jnp.ones((BLK, LANES), BF16), jnp.zeros((BLK, LANES), BF16)
    for g in range(groups):
        for r in range(reps):
            lanes = slice(r * LANES, (r + 1) * LANES)
            masks = []
            for kind in range(2):
                digit = lambda k: digit_ref[2 * kind + k, pl.ds(r * groups + g, 1), :]
                masks.append((jnp.broadcast_to(digit(1), tile) == sub_f).astype(F32))
                spot = jnp.broadcast_to(digit(0), (BLK, LANES)).astype(BF16)
                hot_ref[g, kind * BLK : (kind + 1) * BLK, lanes] = jnp.where(spot == place, one, none)
            mask_ref[g, :, lanes] = jnp.concatenate(masks, axis=0).astype(BF16)

    def folded(tiles, place):
        out = []
        for half in halves:
            x = shifted(tiles[half * side], -place)
            for q in range(1, side):
                x = jnp.where(segment == q, shifted(tiles[half * side + q], q - place), x)
            out.append(x)
        return out

    def along(res, owned):
        work = [jnp.take_along_axis(x, chosen, axis=0) for x, chosen in zip(owned, choose)]
        out = []
        for r in range(reps):
            value = 0.0
            for table, tract in ((res, tracts[0][r]), (work, tracts[1][r])):
                spot = tract & (LANES - 1)
                first, second = (jnp.take_along_axis(x, spot, axis=1) for x in table)
                value += jnp.where(tract < LANES, first, second)
            out.append(value)
        return out

    empty = jnp.zeros((2 * groups, LANES - 2 * BLK), F32)

    def scatter(values, slot):
        for r in range(reps):
            for k, x in enumerate(split3(values[r])):
                part_ref[slot, k, pl.ds(r * groups, groups), :] = x.astype(F32)
        res, work = [], [jnp.zeros(tile, F32)] * groups
        for g in range(groups):
            columns = []
            for r in range(reps):
                mask = mask_ref[g, :, r * LANES : (r + 1) * LANES]
                parts = [
                    jnp.broadcast_to(part_ref[slot, k, pl.ds(r * groups + g, 1), :], (2 * groups, LANES)).astype(BF16)
                    for k in range(3)
                ]
                columns.append(jnp.concatenate([x * mask for x in parts], axis=0))
            sums = dot_nt(jnp.concatenate(columns, axis=1), hot_ref[g])
            sums = sums[: 2 * groups] + sums[2 * groups : 4 * groups] + sums[4 * groups :]
            sums = jnp.concatenate([sums, empty], axis=1)
            res.append(jnp.where(segment == 0, sums[:groups], 0.0))
            for b in range(groups):
                work[b] = work[b] + jnp.where(need[g] == float(b), sums[groups:], 0.0)
        return [x + y for x, y in zip(res, work)]

    def dot(a, b):
        products = [x * y for x, y in zip(a, b)]
        while len(products) > 1:
            products = [x + y for x, y in zip(products[::2], products[1::2])]
        return jnp.sum(jnp.sum(products[0], axis=0, keepdims=True), axis=1, keepdims=True)

    def ratio(a, b):
        return jnp.where(b > 0.0, a / jnp.where(b > 0.0, b, 1.0), 0.0)

    def put(row, value, which):
        for r in which:
            out_ref[pl.ds(r * sent_rows + row, groups, stride=reps * sent_rows), :] = value

    def own_rows(rep):
        return [of_groups(at_own + half, rep) for half in halves]

    def owned(rep, slot):
        return folded(turned(unfold(rep, 0), slot), 0)

    weight = [of_groups(at_base, r) * jnp.exp(x) for r, x in enumerate(along(own_rows(0), owned(1, 0)))]
    v = own_rows(2) + own_rows(3)
    on_jobs = along(own_rows(2), owned(3, 1))
    last = last_on_jobs = None
    sizes, middles, scales, backs = [], [], [], []
    for k in range(ITERS + 1):
        if k:
            q = [x * y for x, y in zip(weight, on_jobs)]
            sizes.append(dot(v, v))
            middles.append(ratio(dot(q, on_jobs), sizes[-1]))
        tiles = scatter(q if k else weight, k)
        rows_of_w = turned(tiles, 2 + k)
        res = folded(rows_of_w, 0)
        w = res + folded(tiles, 1)
        w_on_jobs = along(res, folded(rows_of_w, 1))
        if k:
            square = dot(tiles, tiles)
            scale = jnp.where(square > 0.0, lax.rsqrt(jnp.where(square > 0.0, square, 1.0)), 0.0)
            if last is not None:
                backs.append(ratio(scales[-1] * sizes[-1], sizes[-2]))
            scales.append(square * scale)

            def step(x, y, z):
                out = x - middles[-1] * y
                return scale * (out if z is None else out - backs[-1] * z)

            nothing = [None] * max(len(v), reps)
            following = [step(*t) for t in zip(w, v, last or nothing)]
            following_on_jobs = [step(*t) for t in zip(w_on_jobs, on_jobs, last_on_jobs or nothing)]
            last, last_on_jobs = v, on_jobs
        else:
            following = [y - x for x, y in zip(w, v)]
            following_on_jobs = [y - x for x, y in zip(w_on_jobs, on_jobs)]
        v, on_jobs = following, following_on_jobs
        for part in range(2):
            for half in halves:
                put(2 * k + part, v[part * len(halves) + half], range(half, reps, HALVES))
    numbers = jnp.zeros(tile, F32)
    for k, entry in enumerate(sizes + middles + scales + backs):
        numbers = jnp.where(lane == k, entry, numbers)
    put(sent_rows - 1, numbers, range(reps))
    most = in_ref[pl.ds(at_slot, groups * reps, stride=rows), :]
    flag_ref[0] = (jnp.max(most[:, cap:]) > float(cap)).astype(jnp.int32)


def join_kernel(dims, in_ref, out_ref):
    devices, sent_rows = dims["devices"], dims["sent_rows"]
    tile = (devices, LANES)

    def take(row):
        return in_ref[pl.ds(row, devices, stride=sent_rows), :]

    numbers = take(sent_rows - 1)
    entry = lambda k: jnp.broadcast_to(numbers[:, k : k + 1], tile)
    sizes, middles, scales, backs = ([entry(k * ITERS + j) for j in range(ITERS - (k == 3))] for k in range(4))

    def inner(a, b):
        return jnp.sum(sum(g * (x * y) for g, x, y in zip(sizes, a, b)), axis=0, keepdims=True)

    resid = [jnp.ones(tile, F32)]
    direct = list(resid)
    step = []
    norm = inner(resid, resid)
    for turn in range(ITERS):
        image = []
        for k in range(turn + 2):
            terms = []
            if k:
                terms.append(scales[k - 1] * direct[k - 1])
            if k <= turn:
                terms.append((middles[k] + RIDGE) * direct[k])
            if k < turn:
                terms.append(backs[k] * direct[k + 1])
            image.append(sum(terms))
        alpha = norm / inner(direct, image)
        step = [s + alpha * d for s, d in zip(step, direct)] + [alpha * d for d in direct[len(step) :]]
        resid = [r - alpha * i for r, i in zip(resid, image)] + [-alpha * i for i in image[len(resid) :]]
        if turn + 1 < ITERS:
            following = inner(resid, resid)
            beta = following / norm
            direct = [r + beta * d for r, d in zip(resid, direct)] + resid[len(direct) :]
            norm = following

    for part in range(2):
        vectors = [take(2 * k + part) for k in range(ITERS + 1)]
        out_ref[pl.ds(part * devices, devices), :] = sum(s * v for s, v in zip(step, vectors))
        out_ref[pl.ds((2 + part) * devices, devices), :] = sum(r * v for r, v in zip(resid, vectors))


def place_kernel(dims, own_ref, other_ref, *out_refs):
    devices, cells = dims["devices"], dims["cells"]
    first = lax.axis_index("rep") % HALVES == 0
    for k, out_ref in enumerate(out_refs):
        own, other = own_ref[pl.ds(k * devices, devices), :], other_ref[pl.ds(k * devices, devices), :]
        out_ref[:, :LANES] = jnp.where(first, own, other)[:cells]
        out_ref[:, LANES:] = jnp.where(first, other, own)[:cells]


def plan_dims(mesh_shape, shapes):
    groups, reps = mesh_shape["geo"], mesh_shape["rep"]
    cells, tracts = shapes["lam"]
    listed = shapes["needed"][1] * shapes["needed"][2]
    slots = listed * BLK
    jobs = shapes["jobs"]
    cap = LANES - listed
    rows = 5
    fits = (
        groups * reps >= cells
        and reps == 4
        and groups == 8
        and listed == groups
        and tracts == groups * BLK == HALVES * LANES
        and 3 * jobs <= 2 * cells * cap
        and jobs % 256 == 0
    )
    return fits, dict(
        devices=groups * reps,
        groups=groups,
        reps=reps,
        cells=cells,
        tracts=tracts,
        listed=listed,
        cap=cap,
        rows=rows,
        sent_rows=2 * (ITERS + 1) + 1,
    )


def owner_plan(dims, base, job_res, job_slot, job_cell, needed, lam_res, lam_work, target_res, target_work):
    devices, rows, sent_rows, cells, tracts, groups, reps = (
        dims[k] for k in ("devices", "rows", "sent_rows", "cells", "tracts", "groups", "reps")
    )
    vmem = pl.BlockSpec(memory_space=pltpu.VMEM)
    smem = pl.BlockSpec(memory_space=pltpu.SMEM)
    flat = lambda x: in_hbm(x.reshape(1, -1))
    in_hbm = lambda x: pltpu.with_memory_space_constraint(x, pltpu.HBM)
    in_vmem = lambda x: pltpu.with_memory_space_constraint(x, pltpu.VMEM)
    packed = pl.pallas_call(
        functools.partial(pack_kernel, dims),
        out_shape=pltpu.VMEM((devices * rows, LANES), F32),
        in_specs=[smem] + [vmem] * 8,
        out_specs=vmem,
        name="pack",
    )(
        in_hbm(needed.reshape(-1)),
        *map(flat, (base, job_res, job_slot, job_cell)),
        *map(in_hbm, (lam_res, lam_work, target_res, target_work)),
    )
    arrived = lax.all_to_all(packed.reshape(devices, rows, 1, LANES), ALL, split_axis=0, concat_axis=0, tiled=True)
    sent, most = pl.pallas_call(
        functools.partial(cell_kernel, dims),
        out_shape=(
            pltpu.VMEM((devices * sent_rows, LANES), F32),
            pltpu.SMEM((1,), jnp.int32),
        ),
        in_specs=[vmem],
        out_specs=(vmem, smem),
        scratch_shapes=[
            pltpu.VMEM((4, devices, LANES), F32),
            pltpu.VMEM((groups, 2 * groups, reps * LANES), BF16),
            pltpu.VMEM((groups, 2 * BLK, reps * LANES), BF16),
            pltpu.VMEM((ITERS + 1, 3, devices, LANES), F32),
            pltpu.VMEM((2 + ITERS + 1, groups * groups, LANES), F32),
        ],
        name="cell",
    )(in_vmem(arrived.reshape(devices * rows, LANES)))
    sent, over = lax.optimization_barrier((sent, most[0]))
    back = lax.all_to_all(sent.reshape(devices, sent_rows, 1, LANES), ALL, split_axis=0, concat_axis=0, tiled=True)
    own = pl.pallas_call(
        functools.partial(join_kernel, dims),
        out_shape=pltpu.VMEM((4 * devices, LANES), F32),
        in_specs=[vmem],
        out_specs=vmem,
        name="join",
    )(in_vmem(back.reshape(devices * sent_rows, LANES)))
    other = lax.ppermute(own, "rep", [(r, r ^ 1) for r in range(reps)])
    outs = pl.pallas_call(
        functools.partial(place_kernel, dims),
        out_shape=(jax.ShapeDtypeStruct((cells, tracts), F32),) * 4,
        in_specs=[vmem] * 2,
        out_specs=(vmem,) * 4,
        name="place",
    )(in_vmem(own), in_vmem(other))
    return outs, packed, over


def body(mesh_shape, *args):
    base, needed, lam_res = args[0], args[4], args[5]
    shape = needed.shape
    fits, dims = plan_dims(mesh_shape, {"lam": lam_res.shape, "needed": needed.shape, "jobs": base.shape[0]})
    if not fits:
        return start_plan(*args)
    outs, head, over = owner_plan(dims, *args)
    outs, head, over, args = lax.optimization_barrier((outs, head, over, args[:4] + args[5:]))

    def other():
        needed = head[0, dims["cap"] :].astype(jnp.int32).reshape(shape)
        return tuple(start_plan(*args[:4], needed, *args[4:]))

    return lax.cond(over > 0, other, lambda: tuple(outs))


def solution(mesh):
    in_specs = (P(ALL),) * 4 + (P("geo", None, None),) + (P(None, "geo"),) * 4
    out_specs = (P(None, "geo"),) * 4
    return jax.shard_map(
        functools.partial(body, dict(mesh.shape)), mesh=mesh, in_specs=in_specs, out_specs=out_specs, check_vma=False
    )
```

```python
import functools

import jax
import jax.numpy as jnp
from jax import lax
from jax.experimental import pallas as pl
from jax.experimental.pallas import tpu as pltpu
from jax.sharding import PartitionSpec as P

BLK = 32
ITERS = 3
RIDGE = 0.5
LANES = 128
HALVES = 2
ALL = ("geo", "rep")

F32 = jnp.float32
BF16 = jnp.bfloat16


def start_plan(base, job_res, job_slot, job_cell, needed, lam_res, lam_work, target_res, target_work):
    cells, tracts_dev = lam_res.shape
    blocks_dev = tracts_dev // BLK
    requests = lax.all_to_all(needed[0], "geo", split_axis=0, concat_axis=0, tiled=True)
    sources, listed = requests.shape
    onehot = (
        requests[:, :, None] == jnp.arange(blocks_dev, dtype=jnp.int32)[None, None, :]
    ).astype(jnp.float32)
    slot_shape = (sources, listed, cells, BLK)
    slot_count = sources * listed * cells * BLK
    res_index = job_cell * tracts_dev + job_res
    work_index = (job_slot // BLK * cells + job_cell) * BLK + job_slot % BLK

    def serve(table):
        blocks = table.reshape(cells, blocks_dev, BLK).transpose(1, 0, 2)
        return jnp.take(blocks, requests, axis=0)

    def pick(fetched):
        return fetched.reshape(-1)[work_index]

    def fold(arrived):
        return jnp.einsum("skb,skcx->cbx", onehot, arrived, precision=lax.Precision.HIGHEST)

    def totals(values):
        res_part = jax.ops.segment_sum(values, res_index, num_segments=cells * tracts_dev).reshape(
            cells, tracts_dev
        )
        work_part = jax.ops.segment_sum(values, work_index, num_segments=slot_count).reshape(
            slot_shape
        )
        arrived = lax.all_to_all(work_part, "geo", split_axis=0, concat_axis=0, tiled=True)
        folded = fold(arrived)
        return lax.psum((res_part, folded.reshape(cells, tracts_dev)), "rep")

    def inner(a_res, a_work, b_res, b_work):
        return lax.psum(jnp.sum(a_res * b_res) + jnp.sum(a_work * b_work), "geo")

    fetched_lam = lax.all_to_all(serve(lam_work), "geo", split_axis=0, concat_axis=0, tiled=True)
    weight = base * jnp.exp(lam_res.reshape(-1)[res_index] + pick(fetched_lam))
    total_res, total_work = totals(weight)
    resid_res = -(total_res - target_res)
    resid_work = -(total_work - target_work)
    norm = inner(resid_res, resid_work, resid_res, resid_work)
    zeros = jnp.zeros_like(resid_res)

    def turn(_, state):
        step_res, step_work, resid_res, resid_work, dir_res, dir_work, norm_now = state
        dir_piece = lax.all_to_all(serve(dir_work), "geo", split_axis=0, concat_axis=0, tiled=True)
        along = dir_res.reshape(-1)[res_index] + pick(dir_piece)
        image_res, image_work = totals(weight * along)
        image_res = image_res + RIDGE * dir_res
        image_work = image_work + RIDGE * dir_work
        alpha = norm_now / inner(dir_res, dir_work, image_res, image_work)
        step_res = step_res + alpha * dir_res
        step_work = step_work + alpha * dir_work
        resid_res = resid_res - alpha * image_res
        resid_work = resid_work - alpha * image_work
        norm_next = inner(resid_res, resid_work, resid_res, resid_work)
        dir_res = resid_res + norm_next / norm_now * dir_res
        dir_work = resid_work + norm_next / norm_now * dir_work
        return step_res, step_work, resid_res, resid_work, dir_res, dir_work, norm_next

    state = (zeros, zeros, resid_res, resid_work, resid_res, resid_work, norm)
    return lax.fori_loop(0, ITERS, turn, state)[:4]


def split3(x):
    high = x.astype(BF16)
    rest = x - high.astype(F32)
    mid = rest.astype(BF16)
    low = (rest - mid.astype(F32)).astype(BF16)
    return high, mid, low


def dot_nt(a, b):
    return lax.dot_general(a, b, (((1,), (1,)), ((), ())), preferred_element_type=F32)


def dot_nn(a, b):
    return jnp.dot(a, b, preferred_element_type=F32)


def pack_kernel(dims, needed_ref, base_ref, res_ref, slot_ref, cell_ref, a_ref, b_ref, c_ref, d_ref, out_ref):
    devices, rows, cap, listed, cells = dims["devices"], dims["rows"], dims["cap"], dims["listed"], dims["cells"]
    tracts = a_ref.shape[1]
    jobs = cell_ref.shape[1]
    chunk = 256
    cell = cell_ref[...]
    member = lax.broadcasted_iota(jnp.int32, (devices, jobs), 0) == cell
    narrow = lambda x, n: jnp.broadcast_to(x.astype(F32), (n, jobs)).astype(BF16)
    number = lambda n: lax.broadcasted_iota(jnp.int32, (n, jobs), 0).astype(F32).astype(BF16)
    one, none = (lambda n: jnp.ones((n, jobs), BF16)), (lambda n: jnp.zeros((n, jobs), BF16))
    member_n = number(devices) == narrow(cell, devices)
    member_b = jnp.where(member_n, one(devices), none(devices))
    before = lax.broadcasted_iota(jnp.int32, (chunk, chunk), 0) < lax.broadcasted_iota(jnp.int32, (chunk, chunk), 1)
    before = before.astype(F32).astype(BF16)
    ranks = []
    count = jnp.zeros((devices, 1), F32)
    for at in range(0, jobs, chunk):
        part = member_b[:, at : at + chunk]
        seen = dot_nn(part, before) + count
        own = member[:, at : at + chunk]
        ranks.append(jnp.sum(jnp.where(own, seen, 0.0), axis=0, keepdims=True))
        count = count + jnp.sum(own.astype(F32), axis=1, keepdims=True)
    rank = jnp.concatenate(ranks, axis=1).astype(jnp.int32)
    largest = jnp.max(count, axis=0, keepdims=True)
    rank = jnp.where(rank < cap, rank, LANES)
    chosen = jnp.where(number(LANES) == narrow(rank, LANES), one(LANES), none(LANES))
    values = (res_ref[...].astype(F32), slot_ref[...].astype(F32)) + tuple(x.astype(F32) for x in split3(base_ref[...]))
    held = jnp.concatenate([jnp.where(member_n, narrow(value, devices), none(devices)) for value in values], axis=0)
    moved = dot_nt(held, chosen)
    moved = [moved[k * devices : (k + 1) * devices] for k in range(len(values))]
    lane = lax.broadcasted_iota(jnp.int32, (devices, LANES), 1)
    head = jnp.zeros((devices, LANES), F32)
    for p in range(listed):
        head = jnp.where(lane == cap + p, needed_ref[p].astype(F32), head)
    sent = (moved[0] + head, jnp.where(lane < cap, moved[1], largest), moved[2] + moved[3] + moved[4])

    def put(row, value):
        out_ref[pl.ds(row, devices, stride=rows), :] = value

    row = 0
    for value in sent:
        put(row, value)
        row += 1
    rep = lax.axis_index("rep")
    mine = a_ref[...]
    for k, ref in enumerate((b_ref, c_ref, d_ref)):
        mine = jnp.where(rep == k + 1, ref[...], mine)
    mine = jnp.concatenate([mine, jnp.zeros((devices - cells, tracts), F32)], axis=0)
    for at in range(0, tracts, LANES):
        put(row, mine[:, at : at + LANES])
        row += 1


def cell_kernel(dims, in_ref, out_ref, flag_ref, digit_ref, mask_ref, hot_ref, part_ref, turn_ref):
    rows, groups, reps, sent_rows, cap = (dims[k] for k in ("rows", "groups", "reps", "sent_rows", "cap"))
    at_res, at_slot, at_base, at_own = 0, 1, 2, 3
    tile = (groups, LANES)
    side = LANES // BLK
    sub = lax.broadcasted_iota(jnp.int32, tile, 0)
    lane = lax.broadcasted_iota(jnp.int32, tile, 1)
    segment = lane // BLK

    def of_groups(row, rep):
        return in_ref[pl.ds(rep * rows + row, groups, stride=reps * rows), :]

    def shifted(x, segments):
        return pltpu.roll(x, BLK * (segments % side), 1) if segments % side else x

    def unfold(rep, place):
        tiles = []
        for half in range(groups // side):
            x = of_groups(at_own + half, rep)
            tiles += [shifted(x, place - k) for k in range(side)]
        return tiles

    def turned(tiles, slot):
        for b, x in enumerate(tiles):
            turn_ref[slot, pl.ds(b, groups, stride=groups), :] = x
        return [turn_ref[slot, pl.ds(g * groups, groups), :] for g in range(groups)]

    head = of_groups(at_res, 0)
    halves = range(groups // side)
    choose = [jnp.take_along_axis(head, cap + half * side + segment, axis=1).astype(jnp.int32) for half in halves]
    need = []
    for g in range(groups):
        row = jnp.broadcast_to(in_ref[pl.ds(g * reps * rows + at_res, 1), :], tile)
        listed = jnp.sum(jnp.where(lane == cap + sub, row, 0.0), axis=1, keepdims=True)
        need.append(jnp.where(segment == 1, listed, -1.0))

    tracts = [[of_groups(row, r).astype(jnp.int32) for r in range(reps)] for row in (at_res, at_slot)]
    for kind in range(2):
        for r, x in enumerate(tracts[kind]):
            digit_ref[2 * kind, pl.ds(r * groups, groups), :] = (x & (BLK - 1)).astype(F32)
            high = lax.shift_right_logical(x, BLK.bit_length() - 1)
            digit_ref[2 * kind + 1, pl.ds(r * groups, groups), :] = high.astype(F32)

    place = lax.broadcasted_iota(jnp.int32, (BLK, LANES), 0).astype(F32).astype(BF16)
    sub_f = sub.astype(F32)
    one, none = jnp.ones((BLK, LANES), BF16), jnp.zeros((BLK, LANES), BF16)
    for g in range(groups):
        for r in range(reps):
            lanes = slice(r * LANES, (r + 1) * LANES)
            masks = []
            for kind in range(2):
                digit = lambda k: digit_ref[2 * kind + k, pl.ds(r * groups + g, 1), :]
                masks.append((jnp.broadcast_to(digit(1), tile) == sub_f).astype(F32))
                spot = jnp.broadcast_to(digit(0), (BLK, LANES)).astype(BF16)
                hot_ref[g, kind * BLK : (kind + 1) * BLK, lanes] = jnp.where(spot == place, one, none)
            mask_ref[g, :, lanes] = jnp.concatenate(masks, axis=0).astype(BF16)

    def folded(tiles, place):
        out = []
        for half in halves:
            x = shifted(tiles[half * side], -place)
            for q in range(1, side):
                x = jnp.where(segment == q, shifted(tiles[half * side + q], q - place), x)
            out.append(x)
        return out

    def along(res, owned):
        work = [jnp.take_along_axis(x, chosen, axis=0) for x, chosen in zip(owned, choose)]
        out = []
        for r in range(reps):
            value = 0.0
            for table, tract in ((res, tracts[0][r]), (work, tracts[1][r])):
                spot = tract & (LANES - 1)
                first, second = (jnp.take_along_axis(x, spot, axis=1) for x in table)
                value += jnp.where(tract < LANES, first, second)
            out.append(value)
        return out

    empty = jnp.zeros((2 * groups, LANES - 2 * BLK), F32)

    def scatter(values, slot):
        for r in range(reps):
            for k, x in enumerate(split3(values[r])):
                part_ref[slot, k, pl.ds(r * groups, groups), :] = x.astype(F32)
        res, work = [], [jnp.zeros(tile, F32)] * groups
        for g in range(groups):
            columns = []
            for r in range(reps):
                mask = mask_ref[g, :, r * LANES : (r + 1) * LANES]
                parts = [
                    jnp.broadcast_to(part_ref[slot, k, pl.ds(r * groups + g, 1), :], (2 * groups, LANES)).astype(BF16)
                    for k in range(3)
                ]
                columns.append(jnp.concatenate([x * mask for x in parts], axis=0))
            sums = dot_nt(jnp.concatenate(columns, axis=1), hot_ref[g])
            sums = sums[: 2 * groups] + sums[2 * groups : 4 * groups] + sums[4 * groups :]
            sums = jnp.concatenate([sums, empty], axis=1)
            res.append(jnp.where(segment == 0, sums[:groups], 0.0))
            for b in range(groups):
                work[b] = work[b] + jnp.where(need[g] == float(b), sums[groups:], 0.0)
        return [x + y for x, y in zip(res, work)]

    def dot(a, b):
        products = [x * y for x, y in zip(a, b)]
        while len(products) > 1:
            products = [x + y for x, y in zip(products[::2], products[1::2])]
        return jnp.sum(jnp.sum(products[0], axis=0, keepdims=True), axis=1, keepdims=True)

    def ratio(a, b):
        return jnp.where(b > 0.0, a / jnp.where(b > 0.0, b, 1.0), 0.0)

    def put(row, value, which):
        for r in which:
            out_ref[pl.ds(r * sent_rows + row, groups, stride=reps * sent_rows), :] = value

    def own_rows(rep):
        return [of_groups(at_own + half, rep) for half in halves]

    def owned(rep, slot):
        return folded(turned(unfold(rep, 0), slot), 0)

    weight = [of_groups(at_base, r) * jnp.exp(x) for r, x in enumerate(along(own_rows(0), owned(1, 0)))]
    v = own_rows(2) + own_rows(3)
    on_jobs = along(own_rows(2), owned(3, 1))
    last = last_on_jobs = None
    sizes, middles, scales, backs = [], [], [], []
    for k in range(ITERS + 1):
        if k:
            q = [x * y for x, y in zip(weight, on_jobs)]
            sizes.append(dot(v, v))
            middles.append(ratio(dot(q, on_jobs), sizes[-1]))
        tiles = scatter(q if k else weight, k)
        rows_of_w = turned(tiles, 2 + k)
        res = folded(rows_of_w, 0)
        w = res + folded(tiles, 1)
        w_on_jobs = along(res, folded(rows_of_w, 1))
        if k:
            square = dot(tiles, tiles)
            scale = jnp.where(square > 0.0, lax.rsqrt(jnp.where(square > 0.0, square, 1.0)), 0.0)
            if last is not None:
                backs.append(ratio(scales[-1] * sizes[-1], sizes[-2]))
            scales.append(square * scale)

            def step(x, y, z):
                out = x - middles[-1] * y
                return scale * (out if z is None else out - backs[-1] * z)

            nothing = [None] * max(len(v), reps)
            following = [step(*t) for t in zip(w, v, last or nothing)]
            following_on_jobs = [step(*t) for t in zip(w_on_jobs, on_jobs, last_on_jobs or nothing)]
            last, last_on_jobs = v, on_jobs
        else:
            following = [y - x for x, y in zip(w, v)]
            following_on_jobs = [y - x for x, y in zip(w_on_jobs, on_jobs)]
        v, on_jobs = following, following_on_jobs
        for part in range(2):
            for half in halves:
                put(2 * k + part, v[part * len(halves) + half], range(half, reps, HALVES))
    numbers = jnp.zeros(tile, F32)
    for k, entry in enumerate(sizes + middles + scales + backs):
        numbers = jnp.where(lane == k, entry, numbers)
    put(sent_rows - 1, numbers, range(reps))
    most = in_ref[pl.ds(at_slot, groups * reps, stride=rows), :]
    flag_ref[0] = (jnp.max(most[:, cap:]) > float(cap)).astype(jnp.int32)


def join_kernel(dims, in_ref, out_ref):
    devices, sent_rows = dims["devices"], dims["sent_rows"]
    tile = (devices, LANES)

    def take(row):
        return in_ref[pl.ds(row, devices, stride=sent_rows), :]

    numbers = take(sent_rows - 1)
    entry = lambda k: jnp.broadcast_to(numbers[:, k : k + 1], tile)
    sizes, middles, scales, backs = ([entry(k * ITERS + j) for j in range(ITERS - (k == 3))] for k in range(4))

    def inner(a, b):
        return jnp.sum(sum(g * (x * y) for g, x, y in zip(sizes, a, b)), axis=0, keepdims=True)

    resid = [jnp.ones(tile, F32)]
    direct = list(resid)
    step = []
    norm = inner(resid, resid)
    for turn in range(ITERS):
        image = []
        for k in range(turn + 2):
            terms = []
            if k:
                terms.append(scales[k - 1] * direct[k - 1])
            if k <= turn:
                terms.append((middles[k] + RIDGE) * direct[k])
            if k < turn:
                terms.append(backs[k] * direct[k + 1])
            image.append(sum(terms))
        alpha = norm / inner(direct, image)
        step = [s + alpha * d for s, d in zip(step, direct)] + [alpha * d for d in direct[len(step) :]]
        resid = [r - alpha * i for r, i in zip(resid, image)] + [-alpha * i for i in image[len(resid) :]]
        if turn + 1 < ITERS:
            following = inner(resid, resid)
            beta = following / norm
            direct = [r + beta * d for r, d in zip(resid, direct)] + resid[len(direct) :]
            norm = following

    for part in range(2):
        vectors = [take(2 * k + part) for k in range(ITERS + 1)]
        out_ref[pl.ds(part * devices, devices), :] = sum(s * v for s, v in zip(step, vectors))
        out_ref[pl.ds((2 + part) * devices, devices), :] = sum(r * v for r, v in zip(resid, vectors))


def place_kernel(dims, own_ref, other_ref, *out_refs):
    devices, cells = dims["devices"], dims["cells"]
    first = lax.axis_index("rep") % HALVES == 0
    for k, out_ref in enumerate(out_refs):
        own, other = own_ref[pl.ds(k * devices, devices), :], other_ref[pl.ds(k * devices, devices), :]
        out_ref[:, :LANES] = jnp.where(first, own, other)[:cells]
        out_ref[:, LANES:] = jnp.where(first, other, own)[:cells]


def plan_dims(mesh_shape, shapes):
    groups, reps = mesh_shape["geo"], mesh_shape["rep"]
    cells, tracts = shapes["lam"]
    listed = shapes["needed"][1] * shapes["needed"][2]
    slots = listed * BLK
    jobs = shapes["jobs"]
    cap = LANES - listed
    rows = 5
    fits = (
        groups * reps >= cells
        and reps == 4
        and groups == 8
        and listed == groups
        and tracts == groups * BLK == HALVES * LANES
        and 3 * jobs <= 2 * cells * cap
        and jobs % 256 == 0
    )
    return fits, dict(
        devices=groups * reps,
        groups=groups,
        reps=reps,
        cells=cells,
        tracts=tracts,
        listed=listed,
        cap=cap,
        rows=rows,
        sent_rows=2 * (ITERS + 1) + 1,
    )


def owner_plan(dims, base, job_res, job_slot, job_cell, needed, lam_res, lam_work, target_res, target_work):
    devices, rows, sent_rows, cells, tracts, groups, reps = (
        dims[k] for k in ("devices", "rows", "sent_rows", "cells", "tracts", "groups", "reps")
    )
    vmem = pl.BlockSpec(memory_space=pltpu.VMEM)
    smem = pl.BlockSpec(memory_space=pltpu.SMEM)
    flat = lambda x: in_hbm(x.reshape(1, -1))
    in_hbm = lambda x: pltpu.with_memory_space_constraint(x, pltpu.HBM)
    in_vmem = lambda x: pltpu.with_memory_space_constraint(x, pltpu.VMEM)
    packed = pl.pallas_call(
        functools.partial(pack_kernel, dims),
        out_shape=pltpu.VMEM((devices * rows, LANES), F32),
        in_specs=[smem] + [vmem] * 8,
        out_specs=vmem,
        compiler_params=pltpu.CompilerParams(),
        name="pack",
    )(
        in_hbm(needed.reshape(-1)),
        *map(flat, (base, job_res, job_slot, job_cell)),
        *map(in_hbm, (lam_res, lam_work, target_res, target_work)),
    )
    arrived = lax.all_to_all(packed.reshape(devices, rows, 1, LANES), ALL, split_axis=0, concat_axis=0, tiled=True)
    sent, most = pl.pallas_call(
        functools.partial(cell_kernel, dims),
        out_shape=(
            pltpu.VMEM((devices * sent_rows, LANES), F32),
            pltpu.SMEM((1,), jnp.int32),
        ),
        in_specs=[vmem],
        out_specs=(vmem, smem),
        scratch_shapes=[
            pltpu.VMEM((4, devices, LANES), F32),
            pltpu.VMEM((groups, 2 * groups, reps * LANES), BF16),
            pltpu.VMEM((groups, 2 * BLK, reps * LANES), BF16),
            pltpu.VMEM((ITERS + 1, 3, devices, LANES), F32),
            pltpu.VMEM((2 + ITERS + 1, groups * groups, LANES), F32),
        ],
        compiler_params=pltpu.CompilerParams(),
        name="cell",
    )(in_vmem(arrived.reshape(devices * rows, LANES)))
    sent, over = lax.optimization_barrier((sent, most[0]))
    back = lax.all_to_all(sent.reshape(devices, sent_rows, 1, LANES), ALL, split_axis=0, concat_axis=0, tiled=True)
    own = pl.pallas_call(
        functools.partial(join_kernel, dims),
        out_shape=pltpu.VMEM((4 * devices, LANES), F32),
        in_specs=[vmem],
        out_specs=vmem,
        name="join",
    )(in_vmem(back.reshape(devices * sent_rows, LANES)))
    other = lax.ppermute(own, "rep", [(r, r ^ 1) for r in range(reps)])
    outs = pl.pallas_call(
        functools.partial(place_kernel, dims),
        out_shape=(jax.ShapeDtypeStruct((cells, tracts), F32),) * 4,
        in_specs=[vmem] * 2,
        out_specs=(vmem,) * 4,
        name="place",
    )(in_vmem(own), in_vmem(other))
    return outs, packed, over


def body(mesh_shape, *args):
    base, needed, lam_res = args[0], args[4], args[5]
    shape = needed.shape
    fits, dims = plan_dims(mesh_shape, {"lam": lam_res.shape, "needed": needed.shape, "jobs": base.shape[0]})
    if not fits:
        return start_plan(*args)
    outs, head, over = owner_plan(dims, *args)
    outs, head, args = lax.optimization_barrier((outs, head, args[:4] + args[5:]))

    def other():
        needed = head[0, dims["cap"] :].astype(jnp.int32).reshape(shape)
        return tuple(start_plan(*args[:4], needed, *args[4:]))

    return lax.switch(over, (lambda: tuple(outs), other))


def solution(mesh):
    in_specs = (P(ALL),) * 4 + (P("geo", None, None),) + (P(None, "geo"),) * 4
    out_specs = (P(None, "geo"),) * 4
    return jax.shard_map(
        functools.partial(body, dict(mesh.shape)), mesh=mesh, in_specs=in_specs, out_specs=out_specs, check_vma=False
    )
```

```python
import functools

import jax
import jax.numpy as jnp
from jax import lax
from jax.experimental import pallas as pl
from jax.experimental.pallas import tpu as pltpu
from jax.sharding import PartitionSpec as P

BLK = 32
ITERS = 3
RIDGE = 0.5
LANES = 128
HALVES = 2
ALL = ("geo", "rep")
OWNERS = ("rep", "geo")

F32 = jnp.float32
BF16 = jnp.bfloat16


def start_plan(base, job_res, job_slot, job_cell, needed, lam_res, lam_work, target_res, target_work):
    cells, tracts_dev = lam_res.shape
    blocks_dev = tracts_dev // BLK
    requests = lax.all_to_all(needed[0], "geo", split_axis=0, concat_axis=0, tiled=True)
    sources, listed = requests.shape
    onehot = (
        requests[:, :, None] == jnp.arange(blocks_dev, dtype=jnp.int32)[None, None, :]
    ).astype(jnp.float32)
    slot_shape = (sources, listed, cells, BLK)
    slot_count = sources * listed * cells * BLK
    res_index = job_cell * tracts_dev + job_res
    work_index = (job_slot // BLK * cells + job_cell) * BLK + job_slot % BLK

    def serve(table):
        blocks = table.reshape(cells, blocks_dev, BLK).transpose(1, 0, 2)
        return jnp.take(blocks, requests, axis=0)

    def pick(fetched):
        return fetched.reshape(-1)[work_index]

    def fold(arrived):
        return jnp.einsum("skb,skcx->cbx", onehot, arrived, precision=lax.Precision.HIGHEST)

    def totals(values):
        res_part = jax.ops.segment_sum(values, res_index, num_segments=cells * tracts_dev).reshape(
            cells, tracts_dev
        )
        work_part = jax.ops.segment_sum(values, work_index, num_segments=slot_count).reshape(
            slot_shape
        )
        arrived = lax.all_to_all(work_part, "geo", split_axis=0, concat_axis=0, tiled=True)
        folded = fold(arrived)
        return lax.psum((res_part, folded.reshape(cells, tracts_dev)), "rep")

    def inner(a_res, a_work, b_res, b_work):
        return lax.psum(jnp.sum(a_res * b_res) + jnp.sum(a_work * b_work), "geo")

    fetched_lam = lax.all_to_all(serve(lam_work), "geo", split_axis=0, concat_axis=0, tiled=True)
    weight = base * jnp.exp(lam_res.reshape(-1)[res_index] + pick(fetched_lam))
    total_res, total_work = totals(weight)
    resid_res = -(total_res - target_res)
    resid_work = -(total_work - target_work)
    norm = inner(resid_res, resid_work, resid_res, resid_work)
    zeros = jnp.zeros_like(resid_res)

    def turn(_, state):
        step_res, step_work, resid_res, resid_work, dir_res, dir_work, norm_now = state
        dir_piece = lax.all_to_all(serve(dir_work), "geo", split_axis=0, concat_axis=0, tiled=True)
        along = dir_res.reshape(-1)[res_index] + pick(dir_piece)
        image_res, image_work = totals(weight * along)
        image_res = image_res + RIDGE * dir_res
        image_work = image_work + RIDGE * dir_work
        alpha = norm_now / inner(dir_res, dir_work, image_res, image_work)
        step_res = step_res + alpha * dir_res
        step_work = step_work + alpha * dir_work
        resid_res = resid_res - alpha * image_res
        resid_work = resid_work - alpha * image_work
        norm_next = inner(resid_res, resid_work, resid_res, resid_work)
        dir_res = resid_res + norm_next / norm_now * dir_res
        dir_work = resid_work + norm_next / norm_now * dir_work
        return step_res, step_work, resid_res, resid_work, dir_res, dir_work, norm_next

    state = (zeros, zeros, resid_res, resid_work, resid_res, resid_work, norm)
    return lax.fori_loop(0, ITERS, turn, state)[:4]


def split3(x):
    high = x.astype(BF16)
    rest = x - high.astype(F32)
    mid = rest.astype(BF16)
    low = (rest - mid.astype(F32)).astype(BF16)
    return high, mid, low


def dot_nt(a, b):
    return lax.dot_general(a, b, (((1,), (1,)), ((), ())), preferred_element_type=F32)


def dot_nn(a, b):
    return jnp.dot(a, b, preferred_element_type=F32)


def pack_kernel(dims, needed_ref, base_ref, res_ref, slot_ref, cell_ref, a_ref, b_ref, c_ref, d_ref, out_ref):
    devices, rows, cap, listed, cells = dims["devices"], dims["rows"], dims["cap"], dims["listed"], dims["cells"]
    tracts = a_ref.shape[1]
    jobs = cell_ref.shape[1]
    chunk = 256
    cell = cell_ref[...]
    member = lax.broadcasted_iota(jnp.int32, (devices, jobs), 0) == cell
    narrow = lambda x, n: jnp.broadcast_to(x.astype(F32), (n, jobs)).astype(BF16)
    number = lambda n: lax.broadcasted_iota(jnp.int32, (n, jobs), 0).astype(F32).astype(BF16)
    one, none = (lambda n: jnp.ones((n, jobs), BF16)), (lambda n: jnp.zeros((n, jobs), BF16))
    member_n = number(devices) == narrow(cell, devices)
    member_b = jnp.where(member_n, one(devices), none(devices))
    before = lax.broadcasted_iota(jnp.int32, (chunk, chunk), 0) < lax.broadcasted_iota(jnp.int32, (chunk, chunk), 1)
    before = before.astype(F32).astype(BF16)
    ranks = []
    count = jnp.zeros((devices, 1), F32)
    for at in range(0, jobs, chunk):
        part = member_b[:, at : at + chunk]
        seen = dot_nn(part, before) + count
        own = member[:, at : at + chunk]
        ranks.append(jnp.sum(jnp.where(own, seen, 0.0), axis=0, keepdims=True))
        count = count + jnp.sum(own.astype(F32), axis=1, keepdims=True)
    rank = jnp.concatenate(ranks, axis=1).astype(jnp.int32)
    largest = jnp.max(count, axis=0, keepdims=True)
    rank = jnp.where(rank < cap, rank, LANES)
    chosen = jnp.where(number(LANES) == narrow(rank, LANES), one(LANES), none(LANES))
    values = (res_ref[...].astype(F32), slot_ref[...].astype(F32)) + tuple(x.astype(F32) for x in split3(base_ref[...]))
    held = jnp.concatenate([jnp.where(member_n, narrow(value, devices), none(devices)) for value in values], axis=0)
    moved = dot_nt(held, chosen)
    moved = [moved[k * devices : (k + 1) * devices] for k in range(len(values))]
    lane = lax.broadcasted_iota(jnp.int32, (devices, LANES), 1)
    head = jnp.zeros((devices, LANES), F32)
    for p in range(listed):
        head = jnp.where(lane == cap + p, needed_ref[p].astype(F32), head)
    sent = (moved[0] + head, jnp.where(lane < cap, moved[1], largest), moved[2] + moved[3] + moved[4])

    def put(row, value):
        out_ref[pl.ds(row, devices, stride=rows), :] = value

    row = 0
    for value in sent:
        put(row, value)
        row += 1
    rep = lax.axis_index("rep")
    mine = a_ref[...]
    for k, ref in enumerate((b_ref, c_ref, d_ref)):
        mine = jnp.where(rep == k + 1, ref[...], mine)
    mine = jnp.concatenate([mine, jnp.zeros((devices - cells, tracts), F32)], axis=0)
    for at in range(0, tracts, LANES):
        put(row, mine[:, at : at + LANES])
        row += 1


def cell_kernel(dims, in_ref, out_ref, flag_ref, digit_ref, mask_ref, hot_ref, part_ref, turn_ref):
    rows, groups, reps, sent_rows, cap = (dims[k] for k in ("rows", "groups", "reps", "sent_rows", "cap"))
    at_res, at_slot, at_base, at_own = 0, 1, 2, 3
    tile = (groups, LANES)
    side = LANES // BLK
    sub = lax.broadcasted_iota(jnp.int32, tile, 0)
    lane = lax.broadcasted_iota(jnp.int32, tile, 1)
    segment = lane // BLK

    def of_groups(row, rep):
        return in_ref[pl.ds(rep * groups * rows + row, groups, stride=rows), :]

    def shifted(x, segments):
        return pltpu.roll(x, BLK * (segments % side), 1) if segments % side else x

    def unfold(rep, place):
        tiles = []
        for half in range(groups // side):
            x = of_groups(at_own + half, rep)
            tiles += [shifted(x, place - k) for k in range(side)]
        return tiles

    def turned(tiles, slot):
        for b, x in enumerate(tiles):
            turn_ref[slot, pl.ds(b, groups, stride=groups), :] = x
        return [turn_ref[slot, pl.ds(g * groups, groups), :] for g in range(groups)]

    head = of_groups(at_res, 0)
    halves = range(groups // side)
    choose = [jnp.take_along_axis(head, cap + half * side + segment, axis=1).astype(jnp.int32) for half in halves]
    need = []
    for g in range(groups):
        row = jnp.broadcast_to(in_ref[pl.ds(g * rows + at_res, 1), :], tile)
        listed = jnp.sum(jnp.where(lane == cap + sub, row, 0.0), axis=1, keepdims=True)
        need.append(jnp.where(segment == 1, listed, -1.0))

    tracts = [[of_groups(row, r).astype(jnp.int32) for r in range(reps)] for row in (at_res, at_slot)]
    for kind in range(2):
        for r, x in enumerate(tracts[kind]):
            digit_ref[2 * kind, pl.ds(r * groups, groups), :] = (x & (BLK - 1)).astype(F32)
            high = lax.shift_right_logical(x, BLK.bit_length() - 1)
            digit_ref[2 * kind + 1, pl.ds(r * groups, groups), :] = high.astype(F32)

    place = lax.broadcasted_iota(jnp.int32, (BLK, LANES), 0).astype(F32).astype(BF16)
    sub_f = sub.astype(F32)
    one, none = jnp.ones((BLK, LANES), BF16), jnp.zeros((BLK, LANES), BF16)
    for g in range(groups):
        for r in range(reps):
            lanes = slice(r * LANES, (r + 1) * LANES)
            masks = []
            for kind in range(2):
                digit = lambda k: digit_ref[2 * kind + k, pl.ds(r * groups + g, 1), :]
                masks.append((jnp.broadcast_to(digit(1), tile) == sub_f).astype(F32))
                spot = jnp.broadcast_to(digit(0), (BLK, LANES)).astype(BF16)
                hot_ref[g, kind * BLK : (kind + 1) * BLK, lanes] = jnp.where(spot == place, one, none)
            mask_ref[g, :, lanes] = jnp.concatenate(masks, axis=0).astype(BF16)

    def folded(tiles, place):
        out = []
        for half in halves:
            x = shifted(tiles[half * side], -place)
            for q in range(1, side):
                x = jnp.where(segment == q, shifted(tiles[half * side + q], q - place), x)
            out.append(x)
        return out

    def along(res, owned):
        work = [jnp.take_along_axis(x, chosen, axis=0) for x, chosen in zip(owned, choose)]
        out = []
        for r in range(reps):
            value = 0.0
            for table, tract in ((res, tracts[0][r]), (work, tracts[1][r])):
                spot = tract & (LANES - 1)
                first, second = (jnp.take_along_axis(x, spot, axis=1) for x in table)
                value += jnp.where(tract < LANES, first, second)
            out.append(value)
        return out

    empty = jnp.zeros((2 * groups, LANES - 2 * BLK), F32)

    def scatter(values, slot):
        for r in range(reps):
            for k, x in enumerate(split3(values[r])):
                part_ref[slot, k, pl.ds(r * groups, groups), :] = x.astype(F32)
        res, work = [], [jnp.zeros(tile, F32)] * groups
        for g in range(groups):
            columns = []
            for r in range(reps):
                mask = mask_ref[g, :, r * LANES : (r + 1) * LANES]
                parts = [
                    jnp.broadcast_to(part_ref[slot, k, pl.ds(r * groups + g, 1), :], (2 * groups, LANES)).astype(BF16)
                    for k in range(3)
                ]
                columns.append(jnp.concatenate([x * mask for x in parts], axis=0))
            sums = dot_nt(jnp.concatenate(columns, axis=1), hot_ref[g])
            sums = sums[: 2 * groups] + sums[2 * groups : 4 * groups] + sums[4 * groups :]
            sums = jnp.concatenate([sums, empty], axis=1)
            res.append(jnp.where(segment == 0, sums[:groups], 0.0))
            for b in range(groups):
                work[b] = work[b] + jnp.where(need[g] == float(b), sums[groups:], 0.0)
        return [x + y for x, y in zip(res, work)]

    def dot(a, b):
        products = [x * y for x, y in zip(a, b)]
        while len(products) > 1:
            products = [x + y for x, y in zip(products[::2], products[1::2])]
        return jnp.sum(jnp.sum(products[0], axis=0, keepdims=True), axis=1, keepdims=True)

    def ratio(a, b):
        return jnp.where(b > 0.0, a / jnp.where(b > 0.0, b, 1.0), 0.0)

    def put(row, value, which):
        for r in which:
            out_ref[pl.ds(r * groups * sent_rows + row, groups, stride=sent_rows), :] = value

    def own_rows(rep):
        return [of_groups(at_own + half, rep) for half in halves]

    def owned(rep, slot):
        return folded(turned(unfold(rep, 0), slot), 0)

    weight = [of_groups(at_base, r) * jnp.exp(x) for r, x in enumerate(along(own_rows(0), owned(1, 0)))]
    v = own_rows(2) + own_rows(3)
    on_jobs = along(own_rows(2), owned(3, 1))
    last = last_on_jobs = None
    sizes, middles, scales, backs = [], [], [], []
    for k in range(ITERS + 1):
        if k:
            q = [x * y for x, y in zip(weight, on_jobs)]
            sizes.append(dot(v, v))
            middles.append(ratio(dot(q, on_jobs), sizes[-1]))
        tiles = scatter(q if k else weight, k)
        rows_of_w = turned(tiles, 2 + k)
        res = folded(rows_of_w, 0)
        w = res + folded(tiles, 1)
        w_on_jobs = along(res, folded(rows_of_w, 1))
        if k:
            square = dot(tiles, tiles)
            scale = jnp.where(square > 0.0, lax.rsqrt(jnp.where(square > 0.0, square, 1.0)), 0.0)
            if last is not None:
                backs.append(ratio(scales[-1] * sizes[-1], sizes[-2]))
            scales.append(square * scale)

            def step(x, y, z):
                out = x - middles[-1] * y
                return scale * (out if z is None else out - backs[-1] * z)

            nothing = [None] * max(len(v), reps)
            following = [step(*t) for t in zip(w, v, last or nothing)]
            following_on_jobs = [step(*t) for t in zip(w_on_jobs, on_jobs, last_on_jobs or nothing)]
            last, last_on_jobs = v, on_jobs
        else:
            following = [y - x for x, y in zip(w, v)]
            following_on_jobs = [y - x for x, y in zip(w_on_jobs, on_jobs)]
        v, on_jobs = following, following_on_jobs
        for part in range(2):
            for half in halves:
                put(2 * k + part, v[part * len(halves) + half], range(half, reps, HALVES))
    numbers = jnp.zeros(tile, F32)
    for k, entry in enumerate(sizes + middles + scales + backs):
        numbers = jnp.where(lane == k, entry, numbers)
    put(sent_rows - 1, numbers, range(reps))
    most = in_ref[pl.ds(at_slot, groups * reps, stride=rows), :]
    flag_ref[0] = (jnp.max(most[:, cap:]) > float(cap)).astype(jnp.int32)


def join_kernel(dims, in_ref, out_ref):
    devices, sent_rows = dims["devices"], dims["sent_rows"]
    tile = (devices, LANES)

    def take(row):
        return in_ref[pl.ds(row, devices, stride=sent_rows), :]

    numbers = take(sent_rows - 1)
    entry = lambda k: jnp.broadcast_to(numbers[:, k : k + 1], tile)
    sizes, middles, scales, backs = ([entry(k * ITERS + j) for j in range(ITERS - (k == 3))] for k in range(4))

    def inner(a, b):
        return jnp.sum(sum(g * (x * y) for g, x, y in zip(sizes, a, b)), axis=0, keepdims=True)

    resid = [jnp.ones(tile, F32)]
    direct = list(resid)
    step = []
    norm = inner(resid, resid)
    for turn in range(ITERS):
        image = []
        for k in range(turn + 2):
            terms = []
            if k:
                terms.append(scales[k - 1] * direct[k - 1])
            if k <= turn:
                terms.append((middles[k] + RIDGE) * direct[k])
            if k < turn:
                terms.append(backs[k] * direct[k + 1])
            image.append(sum(terms))
        alpha = norm / inner(direct, image)
        step = [s + alpha * d for s, d in zip(step, direct)] + [alpha * d for d in direct[len(step) :]]
        resid = [r - alpha * i for r, i in zip(resid, image)] + [-alpha * i for i in image[len(resid) :]]
        if turn + 1 < ITERS:
            following = inner(resid, resid)
            beta = following / norm
            direct = [r + beta * d for r, d in zip(resid, direct)] + resid[len(direct) :]
            norm = following

    for part in range(2):
        vectors = [take(2 * k + part) for k in range(ITERS + 1)]
        out_ref[pl.ds(part * devices, devices), :] = sum(s * v for s, v in zip(step, vectors))
        out_ref[pl.ds((2 + part) * devices, devices), :] = sum(r * v for r, v in zip(resid, vectors))


def place_kernel(dims, own_ref, other_ref, *out_refs):
    devices, cells = dims["devices"], dims["cells"]
    first = lax.axis_index("rep") % HALVES == 0
    for k, out_ref in enumerate(out_refs):
        own, other = own_ref[pl.ds(k * devices, devices), :], other_ref[pl.ds(k * devices, devices), :]
        out_ref[:, :LANES] = jnp.where(first, own, other)[:cells]
        out_ref[:, LANES:] = jnp.where(first, other, own)[:cells]


def plan_dims(mesh_shape, shapes):
    groups, reps = mesh_shape["geo"], mesh_shape["rep"]
    cells, tracts = shapes["lam"]
    listed = shapes["needed"][1] * shapes["needed"][2]
    slots = listed * BLK
    jobs = shapes["jobs"]
    cap = LANES - listed
    rows = 5
    fits = (
        groups * reps >= cells
        and reps == 4
        and groups == 8
        and listed == groups
        and tracts == groups * BLK == HALVES * LANES
        and 3 * jobs <= 2 * cells * cap
        and jobs % 256 == 0
    )
    return fits, dict(
        devices=groups * reps,
        groups=groups,
        reps=reps,
        cells=cells,
        tracts=tracts,
        listed=listed,
        cap=cap,
        rows=rows,
        sent_rows=2 * (ITERS + 1) + 1,
    )


def owner_plan(dims, base, job_res, job_slot, job_cell, needed, lam_res, lam_work, target_res, target_work):
    devices, rows, sent_rows, cells, tracts, groups, reps = (
        dims[k] for k in ("devices", "rows", "sent_rows", "cells", "tracts", "groups", "reps")
    )
    vmem = pl.BlockSpec(memory_space=pltpu.VMEM)
    smem = pl.BlockSpec(memory_space=pltpu.SMEM)
    flat = lambda x: in_hbm(x.reshape(1, -1))
    in_hbm = lambda x: pltpu.with_memory_space_constraint(x, pltpu.HBM)
    in_vmem = lambda x: pltpu.with_memory_space_constraint(x, pltpu.VMEM)
    packed = pl.pallas_call(
        functools.partial(pack_kernel, dims),
        out_shape=pltpu.VMEM((devices * rows, LANES), F32),
        in_specs=[smem] + [vmem] * 8,
        out_specs=vmem,
        compiler_params=pltpu.CompilerParams(),
        name="pack",
    )(
        in_hbm(needed.reshape(-1)),
        *map(flat, (base, job_res, job_slot, job_cell)),
        *map(in_hbm, (lam_res, lam_work, target_res, target_work)),
    )
    arrived = lax.all_to_all(packed.reshape(devices, rows, 1, LANES), OWNERS, split_axis=0, concat_axis=0, tiled=True)
    sent, most = pl.pallas_call(
        functools.partial(cell_kernel, dims),
        out_shape=(
            pltpu.VMEM((devices * sent_rows, LANES), F32),
            pltpu.SMEM((1,), jnp.int32),
        ),
        in_specs=[vmem],
        out_specs=(vmem, smem),
        scratch_shapes=[
            pltpu.VMEM((4, devices, LANES), F32),
            pltpu.VMEM((groups, 2 * groups, reps * LANES), BF16),
            pltpu.VMEM((groups, 2 * BLK, reps * LANES), BF16),
            pltpu.VMEM((ITERS + 1, 3, devices, LANES), F32),
            pltpu.VMEM((2 + ITERS + 1, groups * groups, LANES), F32),
        ],
        compiler_params=pltpu.CompilerParams(),
        name="cell",
    )(in_vmem(arrived.reshape(devices * rows, LANES)))
    sent, over = lax.optimization_barrier((sent, most[0]))
    back = lax.all_to_all(sent.reshape(devices, sent_rows, 1, LANES), OWNERS, split_axis=0, concat_axis=0, tiled=True)
    own = pl.pallas_call(
        functools.partial(join_kernel, dims),
        out_shape=pltpu.VMEM((4 * devices, LANES), F32),
        in_specs=[vmem],
        out_specs=vmem,
        name="join",
    )(in_vmem(back.reshape(devices * sent_rows, LANES)))
    other = lax.ppermute(own, "rep", [(r, r ^ 1) for r in range(reps)])
    outs = pl.pallas_call(
        functools.partial(place_kernel, dims),
        out_shape=(jax.ShapeDtypeStruct((cells, tracts), F32),) * 4,
        in_specs=[vmem] * 2,
        out_specs=(vmem,) * 4,
        name="place",
    )(in_vmem(own), in_vmem(other))
    return outs, packed, over


def body(mesh_shape, *args):
    base, needed, lam_res = args[0], args[4], args[5]
    shape = needed.shape
    fits, dims = plan_dims(mesh_shape, {"lam": lam_res.shape, "needed": needed.shape, "jobs": base.shape[0]})
    if not fits:
        return start_plan(*args)
    outs, head, over = owner_plan(dims, *args)
    outs, head, args = lax.optimization_barrier((outs, head, args[:4] + args[5:]))

    def other():
        needed = head[0, dims["cap"] :].astype(jnp.int32).reshape(shape)
        return tuple(start_plan(*args[:4], needed, *args[4:]))

    return lax.switch(over, (lambda: tuple(outs), other))


def solution(mesh):
    in_specs = (P(ALL),) * 4 + (P("geo", None, None),) + (P(None, "geo"),) * 4
    out_specs = (P(None, "geo"),) * 4
    return jax.shard_map(
        functools.partial(body, dict(mesh.shape)), mesh=mesh, in_specs=in_specs, out_specs=out_specs, check_vma=False
    )
```

```python
import functools

import jax
import jax.numpy as jnp
from jax import lax
from jax.experimental import pallas as pl
from jax.experimental.pallas import tpu as pltpu
from jax.sharding import PartitionSpec as P

BLK = 32
ITERS = 3
RIDGE = 0.5
LANES = 128
HALVES = 2
ALL = ("geo", "rep")
OWNERS = ("rep", "geo")

F32 = jnp.float32
BF16 = jnp.bfloat16


def start_plan(base, job_res, job_slot, job_cell, needed, lam_res, lam_work, target_res, target_work):
    cells, tracts_dev = lam_res.shape
    blocks_dev = tracts_dev // BLK
    requests = lax.all_to_all(needed[0], "geo", split_axis=0, concat_axis=0, tiled=True)
    sources, listed = requests.shape
    onehot = (
        requests[:, :, None] == jnp.arange(blocks_dev, dtype=jnp.int32)[None, None, :]
    ).astype(jnp.float32)
    slot_shape = (sources, listed, cells, BLK)
    slot_count = sources * listed * cells * BLK
    res_index = job_cell * tracts_dev + job_res
    work_index = (job_slot // BLK * cells + job_cell) * BLK + job_slot % BLK

    def serve(table):
        blocks = table.reshape(cells, blocks_dev, BLK).transpose(1, 0, 2)
        return jnp.take(blocks, requests, axis=0)

    def pick(fetched):
        return fetched.reshape(-1)[work_index]

    def fold(arrived):
        return jnp.einsum("skb,skcx->cbx", onehot, arrived, precision=lax.Precision.HIGHEST)

    def totals(values):
        res_part = jax.ops.segment_sum(values, res_index, num_segments=cells * tracts_dev).reshape(
            cells, tracts_dev
        )
        work_part = jax.ops.segment_sum(values, work_index, num_segments=slot_count).reshape(
            slot_shape
        )
        arrived = lax.all_to_all(work_part, "geo", split_axis=0, concat_axis=0, tiled=True)
        folded = fold(arrived)
        return lax.psum((res_part, folded.reshape(cells, tracts_dev)), "rep")

    def inner(a_res, a_work, b_res, b_work):
        return lax.psum(jnp.sum(a_res * b_res) + jnp.sum(a_work * b_work), "geo")

    fetched_lam = lax.all_to_all(serve(lam_work), "geo", split_axis=0, concat_axis=0, tiled=True)
    weight = base * jnp.exp(lam_res.reshape(-1)[res_index] + pick(fetched_lam))
    total_res, total_work = totals(weight)
    resid_res = -(total_res - target_res)
    resid_work = -(total_work - target_work)
    norm = inner(resid_res, resid_work, resid_res, resid_work)
    zeros = jnp.zeros_like(resid_res)

    def turn(_, state):
        step_res, step_work, resid_res, resid_work, dir_res, dir_work, norm_now = state
        dir_piece = lax.all_to_all(serve(dir_work), "geo", split_axis=0, concat_axis=0, tiled=True)
        along = dir_res.reshape(-1)[res_index] + pick(dir_piece)
        image_res, image_work = totals(weight * along)
        image_res = image_res + RIDGE * dir_res
        image_work = image_work + RIDGE * dir_work
        alpha = norm_now / inner(dir_res, dir_work, image_res, image_work)
        step_res = step_res + alpha * dir_res
        step_work = step_work + alpha * dir_work
        resid_res = resid_res - alpha * image_res
        resid_work = resid_work - alpha * image_work
        norm_next = inner(resid_res, resid_work, resid_res, resid_work)
        dir_res = resid_res + norm_next / norm_now * dir_res
        dir_work = resid_work + norm_next / norm_now * dir_work
        return step_res, step_work, resid_res, resid_work, dir_res, dir_work, norm_next

    state = (zeros, zeros, resid_res, resid_work, resid_res, resid_work, norm)
    return lax.fori_loop(0, ITERS, turn, state)[:4]


def split3(x):
    high = x.astype(BF16)
    rest = x - high.astype(F32)
    mid = rest.astype(BF16)
    low = (rest - mid.astype(F32)).astype(BF16)
    return high, mid, low


def dot_nt(a, b):
    return lax.dot_general(a, b, (((1,), (1,)), ((), ())), preferred_element_type=F32)


def dot_nn(a, b):
    return jnp.dot(a, b, preferred_element_type=F32)


def pack_kernel(dims, needed_ref, base_ref, res_ref, slot_ref, cell_ref, a_ref, b_ref, c_ref, d_ref, out_ref):
    devices, rows, cap, listed, cells = dims["devices"], dims["rows"], dims["cap"], dims["listed"], dims["cells"]
    tracts = a_ref.shape[1]
    jobs = cell_ref.shape[1]
    chunk = 256
    cell = cell_ref[...]
    member = lax.broadcasted_iota(jnp.int32, (devices, jobs), 0) == cell
    narrow = lambda x, n: jnp.broadcast_to(x.astype(F32), (n, jobs)).astype(BF16)
    number = lambda n: lax.broadcasted_iota(jnp.int32, (n, jobs), 0).astype(F32).astype(BF16)
    one, none = (lambda n: jnp.ones((n, jobs), BF16)), (lambda n: jnp.zeros((n, jobs), BF16))
    member_b = jnp.where(number(devices) == narrow(cell, devices), one(devices), none(devices))
    before = lax.broadcasted_iota(jnp.int32, (chunk, chunk), 0) < lax.broadcasted_iota(jnp.int32, (chunk, chunk), 1)
    before = before.astype(F32).astype(BF16)
    ranks = []
    count = jnp.zeros((devices, 1), F32)
    for at in range(0, jobs, chunk):
        part = member_b[:, at : at + chunk]
        seen = dot_nn(part, before) + count
        own = member[:, at : at + chunk]
        ranks.append(jnp.sum(jnp.where(own, seen, 0.0), axis=0, keepdims=True))
        count = count + jnp.sum(own.astype(F32), axis=1, keepdims=True)
    rank = jnp.concatenate(ranks, axis=1).astype(jnp.int32)
    largest = jnp.max(count, axis=0, keepdims=True)
    rank = jnp.where(rank < cap, rank, LANES)
    chosen = jnp.where(number(LANES) == narrow(rank, LANES), one(LANES), none(LANES))
    values = (res_ref[...].astype(F32), slot_ref[...].astype(F32)) + tuple(x.astype(F32) for x in split3(base_ref[...]))
    held = jnp.concatenate([jnp.where(member, value, 0.0).astype(BF16) for value in values], axis=0)
    moved = dot_nt(held, chosen)
    moved = [moved[k * devices : (k + 1) * devices] for k in range(len(values))]
    lane = lax.broadcasted_iota(jnp.int32, (devices, LANES), 1)
    head = jnp.zeros((devices, LANES), F32)
    for p in range(listed):
        head = jnp.where(lane == cap + p, needed_ref[p].astype(F32), head)
    sent = (moved[0] + head, jnp.where(lane < cap, moved[1], largest), moved[2] + moved[3] + moved[4])

    def put(row, value):
        out_ref[pl.ds(row, devices, stride=rows), :] = value

    row = 0
    for value in sent:
        put(row, value)
        row += 1
    rep = lax.axis_index("rep")
    mine = a_ref[...]
    for k, ref in enumerate((b_ref, c_ref, d_ref)):
        mine = jnp.where(rep == k + 1, ref[...], mine)
    mine = jnp.concatenate([mine, jnp.zeros((devices - cells, tracts), F32)], axis=0)
    for at in range(0, tracts, LANES):
        put(row, mine[:, at : at + LANES])
        row += 1


def cell_kernel(dims, in_ref, out_ref, flag_ref, digit_ref, mask_ref, hot_ref, part_ref, turn_ref):
    rows, groups, reps, sent_rows, cap = (dims[k] for k in ("rows", "groups", "reps", "sent_rows", "cap"))
    at_res, at_slot, at_base, at_own = 0, 1, 2, 3
    tile = (groups, LANES)
    side = LANES // BLK
    sub = lax.broadcasted_iota(jnp.int32, tile, 0)
    lane = lax.broadcasted_iota(jnp.int32, tile, 1)
    segment = lane // BLK

    def of_groups(row, rep):
        return in_ref[pl.ds(rep * groups * rows + row, groups, stride=rows), :]

    def shifted(x, segments):
        return pltpu.roll(x, BLK * (segments % side), 1) if segments % side else x

    def unfold(rep, place):
        tiles = []
        for half in range(groups // side):
            x = of_groups(at_own + half, rep)
            tiles += [shifted(x, place - k) for k in range(side)]
        return tiles

    def turned(tiles, slot):
        for b, x in enumerate(tiles):
            turn_ref[slot, pl.ds(b, groups, stride=groups), :] = x
        return [turn_ref[slot, pl.ds(g * groups, groups), :] for g in range(groups)]

    head = of_groups(at_res, 0)
    halves = range(groups // side)
    choose = [jnp.take_along_axis(head, cap + half * side + segment, axis=1).astype(jnp.int32) for half in halves]
    need = []
    for g in range(groups):
        row = jnp.broadcast_to(in_ref[pl.ds(g * rows + at_res, 1), :], tile)
        listed = jnp.sum(jnp.where(lane == cap + sub, row, 0.0), axis=1, keepdims=True)
        need.append(jnp.where(segment == 1, listed, -1.0))

    tracts = [[of_groups(row, r).astype(jnp.int32) for r in range(reps)] for row in (at_res, at_slot)]
    for kind in range(2):
        for r, x in enumerate(tracts[kind]):
            digit_ref[2 * kind, pl.ds(r * groups, groups), :] = (x & (BLK - 1)).astype(F32)
            high = lax.shift_right_logical(x, BLK.bit_length() - 1)
            digit_ref[2 * kind + 1, pl.ds(r * groups, groups), :] = high.astype(F32)

    place = lax.broadcasted_iota(jnp.int32, (BLK, LANES), 0).astype(F32).astype(BF16)
    sub_f = sub.astype(F32)
    one, none = jnp.ones((BLK, LANES), BF16), jnp.zeros((BLK, LANES), BF16)
    for g in range(groups):
        for r in range(reps):
            lanes = slice(r * LANES, (r + 1) * LANES)
            masks = []
            for kind in range(2):
                digit = lambda k: digit_ref[2 * kind + k, pl.ds(r * groups + g, 1), :]
                masks.append((jnp.broadcast_to(digit(1), tile) == sub_f).astype(F32))
                spot = jnp.broadcast_to(digit(0), (BLK, LANES)).astype(BF16)
                hot_ref[g, kind * BLK : (kind + 1) * BLK, lanes] = jnp.where(spot == place, one, none)
            mask_ref[g, :, lanes] = jnp.concatenate(masks, axis=0).astype(BF16)

    def folded(tiles, place):
        out = []
        for half in halves:
            x = shifted(tiles[half * side], -place)
            for q in range(1, side):
                x = jnp.where(segment == q, shifted(tiles[half * side + q], q - place), x)
            out.append(x)
        return out

    def along(res, owned):
        work = [jnp.take_along_axis(x, chosen, axis=0) for x, chosen in zip(owned, choose)]
        out = []
        for r in range(reps):
            value = 0.0
            for table, tract in ((res, tracts[0][r]), (work, tracts[1][r])):
                spot = tract & (LANES - 1)
                first, second = (jnp.take_along_axis(x, spot, axis=1) for x in table)
                value += jnp.where(tract < LANES, first, second)
            out.append(value)
        return out

    empty = jnp.zeros((2 * groups, LANES - 2 * BLK), F32)

    def scatter(values, slot):
        for r in range(reps):
            for k, x in enumerate(split3(values[r])):
                part_ref[slot, k, pl.ds(r * groups, groups), :] = x.astype(F32)
        res, work = [], [jnp.zeros(tile, F32)] * groups
        for g in range(groups):
            columns = []
            for r in range(reps):
                mask = mask_ref[g, :, r * LANES : (r + 1) * LANES]
                parts = [
                    jnp.broadcast_to(part_ref[slot, k, pl.ds(r * groups + g, 1), :], (2 * groups, LANES)).astype(BF16)
                    for k in range(3)
                ]
                columns.append(jnp.concatenate([x * mask for x in parts], axis=0))
            sums = dot_nt(jnp.concatenate(columns, axis=1), hot_ref[g])
            sums = sums[: 2 * groups] + sums[2 * groups : 4 * groups] + sums[4 * groups :]
            sums = jnp.concatenate([sums, empty], axis=1)
            res.append(jnp.where(segment == 0, sums[:groups], 0.0))
            for b in range(groups):
                work[b] = work[b] + jnp.where(need[g] == float(b), sums[groups:], 0.0)
        return [x + y for x, y in zip(res, work)]

    def dot(a, b):
        products = [x * y for x, y in zip(a, b)]
        while len(products) > 1:
            products = [x + y for x, y in zip(products[::2], products[1::2])]
        return jnp.sum(jnp.sum(products[0], axis=0, keepdims=True), axis=1, keepdims=True)

    def ratio(a, b):
        return jnp.where(b > 0.0, a / jnp.where(b > 0.0, b, 1.0), 0.0)

    def put(row, value, which):
        for r in which:
            out_ref[pl.ds(r * groups * sent_rows + row, groups, stride=sent_rows), :] = value

    def own_rows(rep):
        return [of_groups(at_own + half, rep) for half in halves]

    def owned(rep, slot):
        return folded(turned(unfold(rep, 0), slot), 0)

    weight = [of_groups(at_base, r) * jnp.exp(x) for r, x in enumerate(along(own_rows(0), owned(1, 0)))]
    v = own_rows(2) + own_rows(3)
    on_jobs = along(own_rows(2), owned(3, 1))
    last = last_on_jobs = None
    sizes, middles, scales, backs = [], [], [], []
    for k in range(ITERS + 1):
        if k:
            q = [x * y for x, y in zip(weight, on_jobs)]
            sizes.append(dot(v, v))
            middles.append(ratio(dot(q, on_jobs), sizes[-1]))
        tiles = scatter(q if k else weight, k)
        rows_of_w = turned(tiles, 2 + k)
        res = folded(rows_of_w, 0)
        w = res + folded(tiles, 1)
        w_on_jobs = along(res, folded(rows_of_w, 1))
        if k:
            square = dot(tiles, tiles)
            scale = jnp.where(square > 0.0, lax.rsqrt(jnp.where(square > 0.0, square, 1.0)), 0.0)
            if last is not None:
                backs.append(ratio(scales[-1] * sizes[-1], sizes[-2]))
            scales.append(square * scale)

            def step(x, y, z):
                out = x - middles[-1] * y
                return scale * (out if z is None else out - backs[-1] * z)

            nothing = [None] * max(len(v), reps)
            following = [step(*t) for t in zip(w, v, last or nothing)]
            following_on_jobs = [step(*t) for t in zip(w_on_jobs, on_jobs, last_on_jobs or nothing)]
            last, last_on_jobs = v, on_jobs
        else:
            following = [y - x for x, y in zip(w, v)]
            following_on_jobs = [y - x for x, y in zip(w_on_jobs, on_jobs)]
        v, on_jobs = following, following_on_jobs
        for part in range(2):
            for half in halves:
                put(2 * k + part, v[part * len(halves) + half], range(half, reps, HALVES))
    numbers = jnp.zeros(tile, F32)
    for k, entry in enumerate(sizes + middles + scales + backs):
        numbers = jnp.where(lane == k, entry, numbers)
    put(sent_rows - 1, numbers, range(reps))
    most = in_ref[pl.ds(at_slot, groups * reps, stride=rows), :]
    flag_ref[0] = (jnp.max(most[:, cap:]) > float(cap)).astype(jnp.int32)


def join_kernel(dims, in_ref, out_ref):
    devices, sent_rows = dims["devices"], dims["sent_rows"]
    tile = (devices, LANES)

    def take(row):
        return in_ref[pl.ds(row, devices, stride=sent_rows), :]

    numbers = take(sent_rows - 1)
    entry = lambda k: jnp.broadcast_to(numbers[:, k : k + 1], tile)
    sizes, middles, scales, backs = ([entry(k * ITERS + j) for j in range(ITERS - (k == 3))] for k in range(4))

    def inner(a, b):
        return jnp.sum(sum(g * (x * y) for g, x, y in zip(sizes, a, b)), axis=0, keepdims=True)

    resid = [jnp.ones(tile, F32)]
    direct = list(resid)
    step = []
    norm = inner(resid, resid)
    for turn in range(ITERS):
        image = []
        for k in range(turn + 2):
            terms = []
            if k:
                terms.append(scales[k - 1] * direct[k - 1])
            if k <= turn:
                terms.append((middles[k] + RIDGE) * direct[k])
            if k < turn:
                terms.append(backs[k] * direct[k + 1])
            image.append(sum(terms))
        alpha = norm / inner(direct, image)
        step = [s + alpha * d for s, d in zip(step, direct)] + [alpha * d for d in direct[len(step) :]]
        resid = [r - alpha * i for r, i in zip(resid, image)] + [-alpha * i for i in image[len(resid) :]]
        if turn + 1 < ITERS:
            following = inner(resid, resid)
            beta = following / norm
            direct = [r + beta * d for r, d in zip(resid, direct)] + resid[len(direct) :]
            norm = following

    for part in range(2):
        vectors = [take(2 * k + part) for k in range(ITERS + 1)]
        out_ref[pl.ds(part * devices, devices), :] = sum(s * v for s, v in zip(step, vectors))
        out_ref[pl.ds((2 + part) * devices, devices), :] = sum(r * v for r, v in zip(resid, vectors))


def place_kernel(dims, own_ref, other_ref, *out_refs):
    devices, cells = dims["devices"], dims["cells"]
    first = lax.axis_index("rep") % HALVES == 0
    for k, out_ref in enumerate(out_refs):
        own, other = own_ref[pl.ds(k * devices, devices), :], other_ref[pl.ds(k * devices, devices), :]
        out_ref[:, :LANES] = jnp.where(first, own, other)[:cells]
        out_ref[:, LANES:] = jnp.where(first, other, own)[:cells]


def plan_dims(mesh_shape, shapes):
    groups, reps = mesh_shape["geo"], mesh_shape["rep"]
    cells, tracts = shapes["lam"]
    listed = shapes["needed"][1] * shapes["needed"][2]
    slots = listed * BLK
    jobs = shapes["jobs"]
    cap = LANES - listed
    rows = 5
    fits = (
        groups * reps >= cells
        and reps == 4
        and groups == 8
        and listed == groups
        and tracts == groups * BLK == HALVES * LANES
        and 3 * jobs <= 2 * cells * cap
        and jobs % 256 == 0
    )
    return fits, dict(
        devices=groups * reps,
        groups=groups,
        reps=reps,
        cells=cells,
        tracts=tracts,
        listed=listed,
        cap=cap,
        rows=rows,
        sent_rows=2 * (ITERS + 1) + 1,
    )


def owner_plan(dims, base, job_res, job_slot, job_cell, needed, lam_res, lam_work, target_res, target_work):
    devices, rows, sent_rows, cells, tracts, groups, reps = (
        dims[k] for k in ("devices", "rows", "sent_rows", "cells", "tracts", "groups", "reps")
    )
    vmem = pl.BlockSpec(memory_space=pltpu.VMEM)
    smem = pl.BlockSpec(memory_space=pltpu.SMEM)
    flat = lambda x: in_hbm(x.reshape(1, -1))
    in_hbm = lambda x: pltpu.with_memory_space_constraint(x, pltpu.HBM)
    in_vmem = lambda x: pltpu.with_memory_space_constraint(x, pltpu.VMEM)
    packed = pl.pallas_call(
        functools.partial(pack_kernel, dims),
        out_shape=pltpu.VMEM((devices * rows, LANES), F32),
        in_specs=[smem] + [vmem] * 8,
        out_specs=vmem,
        compiler_params=pltpu.CompilerParams(),
        name="pack",
    )(
        in_hbm(needed.reshape(-1)),
        *map(flat, (base, job_res, job_slot, job_cell)),
        *map(in_hbm, (lam_res, lam_work, target_res, target_work)),
    )
    arrived = lax.all_to_all(packed.reshape(devices, rows, 1, LANES), OWNERS, split_axis=0, concat_axis=0, tiled=True)
    sent, most = pl.pallas_call(
        functools.partial(cell_kernel, dims),
        out_shape=(
            pltpu.VMEM((devices * sent_rows, LANES), F32),
            pltpu.SMEM((1,), jnp.int32),
        ),
        in_specs=[vmem],
        out_specs=(vmem, smem),
        scratch_shapes=[
            pltpu.VMEM((4, devices, LANES), F32),
            pltpu.VMEM((groups, 2 * groups, reps * LANES), BF16),
            pltpu.VMEM((groups, 2 * BLK, reps * LANES), BF16),
            pltpu.VMEM((ITERS + 1, 3, devices, LANES), F32),
            pltpu.VMEM((2 + ITERS + 1, groups * groups, LANES), F32),
        ],
        compiler_params=pltpu.CompilerParams(),
        name="cell",
    )(in_vmem(arrived.reshape(devices * rows, LANES)))
    sent, over = lax.optimization_barrier((sent, most[0]))
    back = lax.all_to_all(sent.reshape(devices, sent_rows, 1, LANES), OWNERS, split_axis=0, concat_axis=0, tiled=True)
    own = pl.pallas_call(
        functools.partial(join_kernel, dims),
        out_shape=pltpu.VMEM((4 * devices, LANES), F32),
        in_specs=[vmem],
        out_specs=vmem,
        name="join",
    )(in_vmem(back.reshape(devices * sent_rows, LANES)))
    other = lax.ppermute(own, "rep", [(r, r ^ 1) for r in range(reps)])
    outs = pl.pallas_call(
        functools.partial(place_kernel, dims),
        out_shape=(jax.ShapeDtypeStruct((cells, tracts), F32),) * 4,
        in_specs=[vmem] * 2,
        out_specs=(vmem,) * 4,
        name="place",
    )(in_vmem(own), in_vmem(other))
    return outs, packed, over


def body(mesh_shape, *args):
    base, needed, lam_res = args[0], args[4], args[5]
    shape = needed.shape
    fits, dims = plan_dims(mesh_shape, {"lam": lam_res.shape, "needed": needed.shape, "jobs": base.shape[0]})
    if not fits:
        return start_plan(*args)
    outs, head, over = owner_plan(dims, *args)
    outs, head, args = lax.optimization_barrier((outs, head, args[:4] + args[5:]))

    def other():
        needed = head[0, dims["cap"] :].astype(jnp.int32).reshape(shape)
        return tuple(start_plan(*args[:4], needed, *args[4:]))

    return lax.switch(over, (lambda: tuple(outs), other))


def solution(mesh):
    in_specs = (P(ALL),) * 4 + (P("geo", None, None),) + (P(None, "geo"),) * 4
    out_specs = (P(None, "geo"),) * 4
    return jax.shard_map(
        functools.partial(body, dict(mesh.shape)), mesh=mesh, in_specs=in_specs, out_specs=out_specs, check_vma=False
    )
```
